512 devices in a mesh: dp: 32 (over x, y), fsdp: 16 (over z, core).
Axes of the slice: x: 4, y: 8, z: 8, core: 2. Of those that a mesh axis runs over, the one named last changes fastest.
Arguments:
- grad_partial: bfloat16 [32, 2, 1024, 8192], P('dp', None, 'fsdp'), may hold values from -0.25 to 0.25
- factors: float32 [32, 1024, 1024], P('dp', 'fsdp'), may hold values from -1 to 11, as said below
- bases: float32 [32, 1024, 1024], P('dp', 'fsdp'), may hold values from -1 to 2, as said below
- first_moment: float32 [32, 1024, 512], P('dp', 'fsdp'), may hold values from -0.3125 to 0.3125
- second_moment: float32 [32, 1024, 512], P('dp', 'fsdp'), may hold values from 0.003 to 0.03
Outputs:
- new_factors: float32 [32, 1024, 1024], P('dp', 'fsdp')
- new_bases: bfloat16 [32, 1024, 1024], P('dp', 'fsdp')
- new_first: float32 [32, 1024, 512], P('dp', 'fsdp')
- new_second: float32 [32, 1024, 512], P('dp', 'fsdp')
- direction: bfloat16 [32, 1024, 512], P('dp', 'fsdp')
The draws below stay inside these ranges and needn't reach their ends.
Inputs may be any that keep to these rules, and one draw needn't show every extreme that they name: Each factors[t] is symmetric and positive definite. Each bases[t] is nonsingular.
All inputs are finite; a program needn't handle non-finite values.
Results may differ from the reference program's by a relative error of at most 0.024.
Values may be sent and summed in bfloat16 or wider, within the bound.
A program may use at most 64 MiB of HBM per device.

```python
import math
import jax
import jax.numpy as jnp
from jax import lax

BLOCK = 1024
CB = 8
RB = 2
COLS = 8192
TASKS = 32
HALF = 512
N_DP = 32


def draw_factors(key, part):
    spread = 0.5
    low_diag = 2.5
    high_diag = 7.0
    amplitude = spread * math.sqrt(3.0) / math.sqrt(BLOCK)
    uniform_noise = jax.random.uniform(jax.random.fold_in(key, 11), (TASKS, BLOCK, BLOCK), jnp.float32, -amplitude, amplitude)
    symmetric = (uniform_noise + jnp.swapaxes(uniform_noise, 1, 2)) / math.sqrt(2.0)
    diagonal = jnp.exp(jax.random.uniform(jax.random.fold_in(key, 12), (TASKS, BLOCK), jnp.float32, math.log(low_diag), math.log(high_diag)))
    return symmetric + diagonal[:, :, None] * jnp.eye(BLOCK, dtype=jnp.float32)[None]


def draw_bases(key, part):
    spread = 0.15
    amplitude = spread * math.sqrt(3.0) / math.sqrt(BLOCK)
    noise_term = jax.random.uniform(jax.random.fold_in(key, 21), (TASKS, BLOCK, BLOCK), jnp.float32, -amplitude, amplitude)
    return noise_term + jnp.eye(BLOCK, dtype=jnp.float32)[None]


def raised(values, rng, source, target, parts, factor):
    owner, partner = [(jnp.arange(values.shape[position]) // (values.shape[position] // parts)).reshape([-1 if axis == position else 1 for axis in range(values.ndim)]) for position in (source, target)]
    chosen = jax.random.permutation(rng, parts)[partner]
    strong = (owner == chosen) | (owner == (partner + parts // 2) % parts)
    return jnp.where(strong, factor * values, values)


def block_levels(own_key, dims, pieces, smallest, largest):
    def one(position, parts):
        steps = jax.random.uniform(jax.random.fold_in(jax.random.fold_in(own_key, 6), position), (parts,), jnp.float32, smallest / len(pieces), largest / len(pieces))
        return jnp.repeat(jnp.exp(steps), dims[position] // parts).reshape((-1,) + (1,) * (len(dims) - position - 1))

    loudness = one(*pieces[0])
    for cut in pieces[1:]:
        loudness = loudness * one(*cut)
    return loudness


def centred(rng, shape, scale, limit, split=(), kind=jnp.bfloat16):
    result = jax.random.normal(rng, shape, jnp.float32) * scale
    if len(split) > 0:
        result = block_levels(rng, shape, split, -0.22, 0.18) * result
    return jnp.clip(result, min=-limit, max=limit).astype(kind)


def noise_with(own_key, extent, width, bound, pieces, heavy, kind=jnp.bfloat16):
    values = width * jax.random.normal(own_key, extent, jnp.float32)
    if pieces:
        values = values * block_levels(own_key, extent, pieces, -0.22, 0.18)
    return jnp.clip(raised(values, jax.random.fold_in(own_key, 3), *heavy), -bound, bound).astype(kind)


def setup_inputs(seed: int = 0) -> dict:
    keys = jax.random.split(jax.random.key(seed), 6)
    return {
        "grad_partial": noise_with(keys[0], (N_DP, RB, BLOCK, COLS), (4.0 / (BLOCK * N_DP) ** 0.5), 0.25, ((0, 32), (2, 16)), (0, 3, 32, 2.75)),
        "factors": draw_factors(jax.random.fold_in(keys[5], 71), 0),
        "bases": draw_bases(jax.random.fold_in(keys[5], 71), 0),
        "first_moment": centred(keys[3], (TASKS, BLOCK, HALF), 0.05, 0.3125, ((0, 32), (1, 16)), jnp.float32),
        "second_moment": jnp.clip(jnp.exp(math.log(0.03) - 2.3025851 * jax.random.uniform(keys[4], (TASKS, BLOCK, HALF), jnp.float32) ** block_levels(keys[4], (TASKS, BLOCK, HALF), ((0, 32), (1, 16)), -0.2, 0.2)), 0.003, 0.03),
    }


def refresh(factor_now, basis_old):
    power_rows = jnp.dot(factor_now.astype(jnp.float32), basis_old.astype(jnp.float32), precision=lax.Precision.HIGHEST, preferred_element_type=jnp.float32)
    gram_matrix = jnp.dot(power_rows.T.astype(jnp.float32), power_rows.astype(jnp.float32), precision=lax.Precision.HIGHEST, preferred_element_type=jnp.float32)
    lower_factor = jnp.linalg.cholesky(gram_matrix)
    solved = lax.linalg.triangular_solve(lower_factor, power_rows, left_side=False, lower=True, transpose_a=True)
    return solved.astype(jnp.bfloat16)

def one_block(arguments):
    block_tile, factor_pair, basis_pair, first_old, second_old = arguments
    left_factor = 0.95 * factor_pair[0] + 0.05 * jnp.dot(block_tile.astype(jnp.float32), block_tile.T.astype(jnp.float32), preferred_element_type=jnp.float32)
    right_factor = 0.95 * factor_pair[1] + 0.05 * jnp.dot(block_tile.T.astype(jnp.float32), block_tile.astype(jnp.float32), preferred_element_type=jnp.float32)
    left_basis = refresh(left_factor, basis_pair[0])
    right_basis = refresh(right_factor, basis_pair[1])
    mixed_rows = jnp.dot(left_basis.T.astype(jnp.float32), block_tile.astype(jnp.float32), preferred_element_type=jnp.float32).astype(jnp.bfloat16)
    rotated = jnp.dot(mixed_rows.astype(jnp.float32), right_basis.astype(jnp.float32), preferred_element_type=jnp.float32)
    rotated = jnp.stack([rotated[:, :HALF], rotated[:, HALF:]])
    first_new = 0.95 * first_old + 0.05 * rotated
    second_new = 0.95 * second_old + 0.05 * rotated * rotated
    normalized = (first_new / (jnp.sqrt(second_new) + 1e-08)).astype(jnp.bfloat16)
    joined = jnp.concatenate([normalized[0], normalized[1]], axis=1)
    weighted = jnp.dot(left_basis.astype(jnp.float32), joined.astype(jnp.float32), preferred_element_type=jnp.float32).astype(jnp.bfloat16)
    combined = jnp.dot(weighted.astype(jnp.float32), right_basis.T.astype(jnp.float32), preferred_element_type=jnp.float32).astype(jnp.bfloat16)
    combined = jnp.stack([combined[:, :HALF], combined[:, HALF:]])
    return (jnp.stack([left_factor, right_factor]), jnp.stack([left_basis, right_basis]), first_new, second_new, combined)

def paired(array_value):
    return array_value.reshape((RB * CB, 2) + array_value.shape[1:])

def unpaired(array_value):
    return array_value.reshape((TASKS,) + array_value.shape[2:])

def reference(grad_partial, factors, bases, first_moment, second_moment):
    summed = lax.optimization_barrier(jnp.sum(grad_partial, axis=0, dtype=jnp.float32)).astype(jnp.bfloat16)
    blocks = summed.reshape(RB, BLOCK, CB, BLOCK).transpose(0, 2, 1, 3).reshape(RB * CB, BLOCK, BLOCK)
    results = lax.map(one_block, (blocks, paired(factors), paired(bases), paired(first_moment), paired(second_moment)))
    return (unpaired(results[0]), unpaired(results[1]), unpaired(results[2]), unpaired(results[3]), unpaired(results[4]))
```

```python
import functools

import jax
import jax.numpy as jnp
from jax import lax
from jax.experimental import pallas as pl
from jax.experimental.pallas import tpu as pltpu
from jax.sharding import PartitionSpec as P

F32 = jnp.float32
BF16 = jnp.bfloat16
NN = (((1,), (0,)), ((), ()))
NT = (((1,), (1,)), ((), ()))
TN = (((0,), (0,)), ((), ()))
NX, NY, NZ = 4, 8, 8
ROWS = 64
BLOCK = 1024
HALF = 512
CHUNKS = 4
CROWS = ROWS // CHUNKS
PANEL = 128
VMEM_SPEC = pl.BlockSpec(memory_space=pltpu.VMEM)
VMEM_BYTES = 60 << 20


def place():
    dp = lax.axis_index("dp")
    fsdp = lax.axis_index("fsdp")
    return dp // NY, lax.rem(dp, NY), fsdp // 2, lax.rem(fsdp, 2)


def remote(src, dst, send, recv, dp, fsdp):
    return pltpu.make_async_remote_copy(
        src_ref=src,
        dst_ref=dst,
        send_sem=send,
        recv_sem=recv,
        device_id={"dp": dp, "fsdp": fsdp},
        device_id_type=pl.DeviceIdType.MESH,
    )


def meet(peers):
    barrier = pltpu.get_barrier_semaphore()
    for dp, fsdp in peers:
        pl.semaphore_signal(
            barrier,
            inc=1,
            device_id={"dp": dp, "fsdp": fsdp},
            device_id_type=pl.DeviceIdType.MESH,
        )
    pl.semaphore_wait(barrier, len(peers))


class Gather:
    def __init__(self, own, held, send, recv, hand_send, hand_recv):
        self.own, self.held = own, held
        self.send, self.recv = send, recv
        self.hand_send, self.hand_recv = hand_send, hand_recv
        self.x, self.y, self.z, self.core = place()
        self.dp = self.x * NY + self.y
        self.started = []

    def slot(self, z, core):
        return lax.rem(z + NZ, NZ) * 2 + core

    def part(self, z, core, step, way):
        view = self.held.at[self.slot(z, core)]
        if step < NZ // 2:
            return view
        return view.at[pl.ds(way * (ROWS // 2), ROWS // 2)]

    def hop(self, step, way):
        sign = 1 - 2 * way
        origin = self.z - sign * (step - 1)
        target = self.slot(self.z + sign, self.core)
        dst = self.part(origin, self.core, step, way)
        src = self.own if step == 1 and self.own is not None else dst
        return remote(
            src, dst, self.send.at[step - 1, way], self.recv.at[step - 1, way], self.dp, target
        )

    def hand(self, item, view, core):
        src = view if item or self.own is None else self.own
        return remote(
            src if core is None else view,
            view,
            self.hand_send.at[item],
            self.hand_recv.at[item],
            self.dp,
            self.slot(self.z, 1 - self.core),
        )

    def begin(self):
        for way in range(2):
            copy = self.hop(1, way)
            copy.start()
            self.started.append(copy)
        copy = self.hand(0, self.part(self.z, self.core, 1, 0), None)
        copy.start()
        self.started.append(copy)

    def advance(self, step):
        for way in range(2):
            sign = 1 - 2 * way
            view = self.part(self.z - sign * step, self.core, step, way)
            remote(
                view,
                view,
                self.send.at[step - 1, way],
                self.recv.at[step - 1, way],
                self.dp,
                self.slot(self.z + sign, self.core),
            ).wait_recv()
            if step < NZ // 2:
                copy = self.hop(step + 1, way)
                copy.start()
                self.started.append(copy)
            copy = self.hand(1 + 2 * (step - 1) + way, view, None)
            copy.start()
            self.started.append(copy)

    def finish(self):
        other = 1 - self.core
        self.hand(0, self.part(self.z, other, 1, 0), other).wait_recv()
        for step in range(1, NZ // 2 + 1):
            for way in range(2):
                sign = 1 - 2 * way
                view = self.part(self.z - sign * step, other, step, way)
                self.hand(1 + 2 * (step - 1) + way, view, other).wait_recv()
        for copy in self.started:
            copy.wait_send()


GATHER_SEMS = (
    pltpu.SemaphoreType.DMA((NZ // 2, 2)),
    pltpu.SemaphoreType.DMA((NZ // 2, 2)),
    pltpu.SemaphoreType.DMA((NZ + 1,)),
    pltpu.SemaphoreType.DMA((NZ + 1,)),
)


def collect_kernel(
    grad, factor, basis, all_grad, all_factor, all_basis,
    first_right, first_left, sum_right, sum_left,
    right_a, right_b, left_a, left_b, lane_sum, lane_in, half_out,
    own_sem,
    s1, r1, s2, r2, s3, r3, ys, yr, ex_send, ex_recv,
    *gather_sems,
):
    x, y, z, core = place()
    me = z * 2 + core
    side = lax.rem(y, 2)
    dp = x * NY + y
    right = lax.rem(x + 1, NX) * NY + y
    left = lax.rem(x + NX - 1, NX) * NY + y
    partner = x * NY + y + 1 - 2 * side
    peers = [(right, me), (left, me)]
    peers += [(x * NY + lax.rem(y + d, NY), me) for d in range(1, NY)]
    peers += [
        (dp, lax.rem(z + 1, NZ) * 2 + core),
        (dp, lax.rem(z + NZ - 1, NZ) * 2 + core),
        (dp, z * 2 + 1 - core),
    ]
    meet(peers)

    def region(owner, part, chunk):
        owner = lax.rem(owner + NX, NX)
        start = pl.multiple_of(lax.rem(owner, 2) * 4096 + part * 2048, 2048)
        return owner // 2, pl.ds(chunk * CROWS, CROWS), pl.ds(start, 2048)

    started = []

    def begin(copy):
        copy.start()
        started.append(copy)
        return copy

    for r in range(CHUNKS):
        begin(remote(grad.at[region(x + 2, 0, r)], first_right.at[r], s1.at[r, 0], r1.at[r, 0], right, me))
        begin(remote(grad.at[region(x - 2, 1, r)], first_left.at[r], s1.at[r, 1], r1.at[r, 1], left, me))
    own_basis = pltpu.make_async_copy(basis, all_basis.at[me], own_sem.at[0])
    own_factor = pltpu.make_async_copy(factor, all_factor.at[me], own_sem.at[1])
    own_basis.start()
    own_factor.start()
    gather_b = Gather(basis, all_basis, *gather_sems[0:4])
    gather_f = Gather(factor, all_factor, *gather_sems[4:8])
    gather_g = Gather(None, all_grad, *gather_sems[8:12])
    gather_b.begin()
    gather_f.begin()

    def forward(r):
        remote(first_right.at[r], first_right.at[r], s1.at[r, 0], r1.at[r, 0], right, me).wait_recv()
        own = grad[region(x + 1, 0, r)].astype(F32)
        sum_right[r] = (own + first_right[r].astype(F32)).astype(BF16)
        begin(remote(sum_right.at[r], right_a.at[r], s2.at[r, 0], r2.at[r, 0], right, me))
        begin(remote(grad.at[region(x + 1, 1, r)], right_b.at[r], s3.at[r, 0], r3.at[r, 0], right, me))
        remote(first_left.at[r], first_left.at[r], s1.at[r, 1], r1.at[r, 1], left, me).wait_recv()
        own = grad[region(x - 1, 1, r)].astype(F32)
        sum_left[r] = (own + first_left[r].astype(F32)).astype(BF16)
        begin(remote(sum_left.at[r], left_b.at[r], s2.at[r, 1], r2.at[r, 1], left, me))
        begin(remote(grad.at[region(x - 1, 0, r)], left_a.at[r], s3.at[r, 1], r3.at[r, 1], left, me))

    def turn(r):
        remote(right_a.at[r], right_a.at[r], s2.at[r, 0], r2.at[r, 0], right, me).wait_recv()
        remote(right_b.at[r], right_b.at[r], s3.at[r, 0], r3.at[r, 0], right, me).wait_recv()
        remote(left_b.at[r], left_b.at[r], s2.at[r, 1], r2.at[r, 1], left, me).wait_recv()
        remote(left_a.at[r], left_a.at[r], s3.at[r, 1], r3.at[r, 1], left, me).wait_recv()
        rows = pl.ds(r * CROWS, CROWS)
        for part, (from_left, from_right) in enumerate(((right_a, left_a), (right_b, left_b))):
            total = grad[region(x, part, r)].astype(F32)
            total = total + from_left[r].astype(F32) + from_right[r].astype(F32)
            total = total.astype(BF16)
            for piece in range(4):
                lane_sum[part * 4 + piece, rows] = total[:, piece * HALF:(piece + 1) * HALF]
        if r % 2:
            send_rows = pl.ds((r - 1) * CROWS, 2 * CROWS)
            for d in range(1, NY):
                target = lax.rem(y + d, NY)
                begin(remote(
                    lane_sum.at[target, send_rows], lane_in.at[d - 1, send_rows],
                    ys.at[d - 1, r // 2], yr.at[d - 1, r // 2], x * NY + target, me,
                ))

    mine = pl.ds(pl.multiple_of(side * HALF, HALF), HALF)
    theirs = pl.ds(pl.multiple_of((1 - side) * HALF, HALF), HALF)

    def land(h):
        rows = pl.ds(2 * h * CROWS, 2 * CROWS)
        total = lane_sum[y, rows].astype(F32)
        for d in range(1, NY):
            view = lane_in.at[d - 1, rows]
            remote(view, view, ys.at[d - 1, h], yr.at[d - 1, h], x * NY + lax.rem(y + d, NY), me).wait_recv()
        for d in range(1, NY):
            total = total + lane_in[d - 1, rows].astype(F32)
        total = total.astype(BF16)
        half_out[rows] = total
        all_grad[me, rows, mine] = total
        begin(remote(half_out.at[rows], all_grad.at[me, rows, mine], ex_send.at[h], ex_recv.at[h], partner, me))

    forward(0)
    forward(1)
    forward(2)
    gather_b.advance(1)
    forward(3)
    gather_f.advance(1)
    turn(0)
    turn(1)
    gather_b.advance(2)
    turn(2)
    gather_f.advance(2)
    turn(3)
    land(0)
    land(1)
    gather_b.advance(3)
    for h in range(2):
        view = all_grad.at[me, pl.ds(2 * h * CROWS, 2 * CROWS), theirs]
        remote(view, view, ex_send.at[h], ex_recv.at[h], partner, me).wait_recv()
    gather_g.begin()
    gather_f.advance(3)
    gather_g.advance(1)
    gather_b.advance(4)
    gather_f.advance(4)
    gather_g.advance(2)
    gather_g.advance(3)
    gather_g.advance(4)
    own_basis.wait()
    own_factor.wait()
    gather_b.finish()
    gather_f.finish()
    gather_g.finish()
    for copy in started:
        copy.wait_send()


def collect(grad, factor, basis):
    slots = 2 * NZ
    chunk = pltpu.VMEM((CHUNKS, CROWS, 2048), BF16)
    dma = pltpu.SemaphoreType.DMA
    return pl.pallas_call(
        collect_kernel,
        out_shape=(
            jax.ShapeDtypeStruct((slots, ROWS, BLOCK), BF16),
            jax.ShapeDtypeStruct((slots, ROWS, BLOCK), BF16),
            jax.ShapeDtypeStruct((slots, ROWS, BLOCK), F32),
        ),
        in_specs=[VMEM_SPEC] * 3,
        out_specs=(VMEM_SPEC,) * 3,
        scratch_shapes=[chunk] * 8
        + [
            pltpu.VMEM((NY, ROWS, HALF), BF16),
            pltpu.VMEM((NY - 1, ROWS, HALF), BF16),
            pltpu.VMEM((ROWS, HALF), BF16),
            dma((2,)),
        ]
        + [dma((CHUNKS, 2))] * 6
        + [dma((NY - 1, 2))] * 2
        + [dma((2,))] * 2
        + list(GATHER_SEMS) * 3,
        compiler_params=pltpu.CompilerParams(
            collective_id=0, has_side_effects=True, vmem_limit_bytes=VMEM_BYTES
        ),
        name="collect",
    )(grad, factor, basis)


def split(value):
    high = value.astype(BF16)
    return high, (value - high.astype(F32)).astype(BF16)


def dot3(left, right, numbers):
    dot = functools.partial(lax.dot_general, dimension_numbers=numbers, preferred_element_type=F32)
    return dot(left[0], right[0]) + (dot(left[0], right[1]) + dot(left[1], right[0]))


def factor_inverse(rows):
    count = len(rows)
    shape = rows[0].shape
    lane = lax.broadcasted_iota(jnp.int32, shape, 1)
    sub = lax.broadcasted_iota(jnp.int32, shape, 0)
    rows = list(rows)
    done = []
    for group in range(count):
        base = 8 * group
        pivot_rows = rows[group]
        columns = [jnp.broadcast_to(pivot_rows[:, base + l:base + l + 1], shape) for l in range(8)]
        result = jnp.zeros(shape, F32)
        for k in range(8):
            own = sub == k
            pivot = jnp.broadcast_to(columns[k][k:k + 1], shape)
            inverse = 1.0 / pivot
            row = jnp.where(lane == base + k, 1.0, jnp.broadcast_to(pivot_rows[k:k + 1], shape))
            result = jnp.where(own, row * lax.rsqrt(pivot), result)
            scale = jnp.where(own, -inverse, columns[k] * inverse)
            pivot_rows = jnp.where(own | (lane == base + k), 0.0, pivot_rows) - scale * row
            for l in range(k + 1, 8):
                columns[l] = jnp.where(own, 0.0, columns[l]) - scale * jnp.broadcast_to(
                    columns[l][k:k + 1], shape
                )
        done.append(jnp.where(lane <= base + sub, result, 0.0))
        if group + 1 < count:
            spread = [jnp.broadcast_to(pivot_rows[l:l + 1], shape) for l in range(8)]
            inside = (lane >= base) & (lane < base + 8)
            for n in range(group + 1, count):
                total = jnp.where(inside, 0.0, rows[n])
                for l in range(8):
                    total = total - jnp.broadcast_to(rows[n][:, base + l:base + l + 1], shape) * spread[l]
                rows[n] = total
    return done


def refresh_kernel(
    grad, factor, basis, own_factor, new_factor, basis_t, new_rows,
    power, high, low, gram, inverse,
):
    x, y, z, core = place()
    me = z * 2 + core
    side = lax.rem(y, 2)
    tile = 256

    @pl.when(side == 0)
    def _():
        @pl.loop(0, BLOCK // tile)
        def _(i):
            rows = pl.ds(pl.multiple_of(i * tile, tile), tile)
            power[rows, :] = lax.dot_general(grad[rows, :], grad[...], NT, preferred_element_type=F32)

    @pl.when(side == 1)
    def _():
        @pl.loop(0, BLOCK // tile)
        def _(i):
            rows = pl.ds(pl.multiple_of(i * tile, tile), tile)
            power[rows, :] = lax.dot_general(grad[:, rows], grad[...], TN, preferred_element_type=F32)

    mine = pl.ds(pl.multiple_of(me * ROWS, ROWS), ROWS)
    new_factor[...] = 0.95 * own_factor[...] + 0.05 * power[mine, :]

    @pl.loop(0, BLOCK // PANEL)
    def _(i):
        rows = pl.ds(pl.multiple_of(i * PANEL, PANEL), PANEL)
        now = 0.95 * factor[rows, :].astype(F32) + 0.05 * power[rows, :]
        high[rows, :], low[rows, :] = split(now)

    @pl.loop(0, BLOCK // tile)
    def _(i):
        rows = pl.ds(pl.multiple_of(i * tile, tile), tile)
        power[rows, :] = dot3(split(basis[:, rows]), (high[...], low[...]), TN)

    @pl.loop(0, BLOCK // PANEL)
    def _(k):
        rows = pl.ds(pl.multiple_of(k * PANEL, PANEL), PANEL)
        panel = split(power[rows, :])
        gram[...] = dot3(panel, panel, NT)
        done = factor_inverse([gram[8 * i:8 * i + 8, :] for i in range(PANEL // 8)])
        for i in range(PANEL // 8):
            inverse[8 * i:8 * i + 8, :] = done[i]
        fresh = dot3(split(inverse[...]), panel, NN)
        basis_t[rows, :] = fresh.astype(BF16)
        fresh = split(fresh)

        @pl.loop(k + 1, BLOCK // PANEL)
        def _(j):
            later = pl.ds(pl.multiple_of(j * PANEL, PANEL), PANEL)
            old = power[later, :]
            overlap = dot3(split(old), fresh, NT)
            power[later, :] = old - dot3(split(overlap), fresh, NN)

    pick = lax.broadcasted_iota(jnp.int32, (ROWS, BLOCK), 1) == me * ROWS + lax.broadcasted_iota(
        jnp.int32, (ROWS, BLOCK), 0
    )
    new_rows[...] = lax.dot_general(
        pick.astype(BF16), basis_t[...], NT, preferred_element_type=F32
    ).astype(BF16)


def refresh(grad, factor, basis, own_factor):
    return pl.pallas_call(
        refresh_kernel,
        out_shape=(
            jax.ShapeDtypeStruct((ROWS, BLOCK), F32),
            jax.ShapeDtypeStruct((BLOCK, BLOCK), BF16),
            jax.ShapeDtypeStruct((ROWS, BLOCK), BF16),
        ),
        in_specs=[VMEM_SPEC] * 4,
        out_specs=(VMEM_SPEC,) * 3,
        scratch_shapes=[
            pltpu.VMEM((BLOCK, BLOCK), F32),
            pltpu.VMEM((BLOCK, BLOCK), BF16),
            pltpu.VMEM((BLOCK, BLOCK), BF16),
            pltpu.VMEM((PANEL, PANEL), F32),
            pltpu.VMEM((PANEL, PANEL), F32),
        ],
        compiler_params=pltpu.CompilerParams(vmem_limit_bytes=VMEM_BYTES),
        name="refresh",
    )(grad, factor, basis, own_factor)


def rotate_kernel(
    basis_t, grad, new_rows, first, second, new_first, new_second, direction,
    mixed, mixed_in, left_rows, part, part_in, normal, all_normal, weighted, weighted_in, turned, turned_in,
    send, recv, *gather_sems,
):
    x, y, z, core = place()
    me = z * 2 + core
    side = lax.rem(y, 2)
    dp = x * NY + y
    partner = dp + 1 - 2 * side
    meet([
        (partner, me),
        (dp, lax.rem(z + 1, NZ) * 2 + core),
        (dp, lax.rem(z + NZ - 1, NZ) * 2 + core),
        (dp, z * 2 + 1 - core),
    ])

    def across(src, dst, i):
        return remote(src, dst, send.at[i], recv.at[i], partner, me)

    def dot(a, b, numbers):
        return lax.dot_general(a, b, numbers, preferred_element_type=F32)

    to_mixed = across(mixed, mixed_in, 0)
    to_rows = across(new_rows, left_rows, 1)
    to_part = across(part, part_in, 2)
    to_weighted = across(weighted, weighted_in, 3)
    to_turned = across(turned, turned_in, 4)
    gather = Gather(normal, all_normal, *gather_sems)
    mine = pl.ds(pl.multiple_of(me * ROWS, ROWS), ROWS)

    @pl.when(side == 0)
    def _():
        mixed[...] = dot(basis_t[mine, :], grad[...], NN).astype(BF16)
        to_mixed.start()
        to_rows.start()
        to_part.wait_recv()

    @pl.when(side == 1)
    def _():
        to_mixed.wait_recv()
        part[...] = dot(mixed_in[...], basis_t[0:HALF, :], NT)
        to_part.start()
        part_in[...] = dot(mixed_in[...], basis_t[HALF:BLOCK, :], NT)

    rotated = part_in[...]
    first_now = 0.95 * first[...] + 0.05 * rotated
    second_now = 0.95 * second[...] + 0.05 * rotated * rotated
    now = (first_now / (jnp.sqrt(second_now) + 1e-08)).astype(BF16)
    normal[...] = now
    all_normal[me] = now
    gather.begin()
    new_first[...] = first_now
    new_second[...] = second_now

    @pl.when(side == 0)
    def _():
        left_rows[...] = new_rows[...]

    @pl.when(side == 1)
    def _():
        to_rows.wait_recv()

    gather.advance(1)
    gather.advance(2)
    gather.advance(3)
    gather.advance(4)
    gather.finish()
    weighted[...] = dot(left_rows[...], all_normal[...].reshape(BLOCK, HALF), NN).astype(BF16)

    @pl.when(side == 0)
    def _():
        to_weighted.start()
        to_turned.wait_recv()
        direction[...] = turned_in[...]
        to_mixed.wait_send()
        to_rows.wait_send()
        to_weighted.wait_send()

    @pl.when(side == 1)
    def _():
        own = dot(weighted[...], basis_t[HALF:BLOCK, :], NN)
        to_weighted.wait_recv()
        total = (own + dot(weighted_in[...], basis_t[0:HALF, :], NN)).astype(BF16)
        turned[...] = total[:, 0:HALF]
        to_turned.start()
        direction[...] = total[:, HALF:BLOCK]
        to_part.wait_send()
        to_turned.wait_send()


def rotate(basis_t, grad, new_rows, first, second):
    dma = pltpu.SemaphoreType.DMA
    return pl.pallas_call(
        rotate_kernel,
        out_shape=(
            jax.ShapeDtypeStruct((ROWS, HALF), F32),
            jax.ShapeDtypeStruct((ROWS, HALF), F32),
            jax.ShapeDtypeStruct((ROWS, HALF), BF16),
        ),
        in_specs=[VMEM_SPEC] * 5,
        out_specs=(VMEM_SPEC,) * 3,
        scratch_shapes=[
            pltpu.VMEM((ROWS, BLOCK), BF16),
            pltpu.VMEM((ROWS, BLOCK), BF16),
            pltpu.VMEM((ROWS, BLOCK), BF16),
            pltpu.VMEM((ROWS, HALF), F32),
            pltpu.VMEM((ROWS, HALF), F32),
            pltpu.VMEM((ROWS, HALF), BF16),
            pltpu.VMEM((2 * NZ, ROWS, HALF), BF16),
            pltpu.VMEM((ROWS, HALF), BF16),
            pltpu.VMEM((ROWS, HALF), BF16),
            pltpu.VMEM((ROWS, HALF), BF16),
            pltpu.VMEM((ROWS, HALF), BF16),
            dma((5,)),
            dma((5,)),
            *GATHER_SEMS,
        ],
        compiler_params=pltpu.CompilerParams(
            collective_id=1, has_side_effects=True, vmem_limit_bytes=VMEM_BYTES
        ),
        name="rotate",
    )(basis_t, grad, new_rows, first, second)


def body(grad_partial, factors, bases, first_moment, second_moment):
    all_grad, all_factor, all_basis = collect(grad_partial[0], factors[0].astype(BF16), bases[0])
    whole = (BLOCK, BLOCK)
    all_grad = all_grad.reshape(whole)
    new_factor, basis_t, new_rows = refresh(
        all_grad, all_factor.reshape(whole), all_basis.reshape(whole), factors[0]
    )
    first_new, second_new, direction = rotate(
        basis_t, all_grad, new_rows, first_moment[0], second_moment[0]
    )
    return (new_factor[None], new_rows[None], first_new[None], second_new[None], direction[None])


def solution(mesh):
    spec = P("dp", "fsdp", None)
    return jax.shard_map(
        body,
        mesh=mesh,
        in_specs=(P("dp", None, "fsdp", None), spec, spec, spec, spec),
        out_specs=(spec,) * 5,
        check_vma=False,
    )
```

```python
import functools

import jax
import jax.numpy as jnp
from jax import lax
from jax.experimental import pallas as pl
from jax.experimental.pallas import tpu as pltpu
from jax.sharding import PartitionSpec as P

F32 = jnp.float32
BF16 = jnp.bfloat16
NN = (((1,), (0,)), ((), ()))
NT = (((1,), (1,)), ((), ()))
TN = (((0,), (0,)), ((), ()))
NX, NY, NZ = 4, 8, 8
ROWS = 64
BLOCK = 1024
HALF = 512
CHUNKS = 4
CROWS = ROWS // CHUNKS
PANEL = 128
VMEM_SPEC = pl.BlockSpec(memory_space=pltpu.VMEM)
VMEM_BYTES = 40 << 20


def place():
    dp = lax.axis_index("dp")
    fsdp = lax.axis_index("fsdp")
    return dp // NY, lax.rem(dp, NY), fsdp // 2, lax.rem(fsdp, 2)


def remote(src, dst, send, recv, dp, fsdp):
    return pltpu.make_async_remote_copy(
        src_ref=src,
        dst_ref=dst,
        send_sem=send,
        recv_sem=recv,
        device_id={"dp": dp, "fsdp": fsdp},
        device_id_type=pl.DeviceIdType.MESH,
    )


def meet(peers):
    barrier = pltpu.get_barrier_semaphore()
    for dp, fsdp in peers:
        pl.semaphore_signal(
            barrier,
            inc=1,
            device_id={"dp": dp, "fsdp": fsdp},
            device_id_type=pl.DeviceIdType.MESH,
        )
    pl.semaphore_wait(barrier, len(peers))


class Gather:
    def __init__(self, own, held, send, recv, hand_send, hand_recv, start=0, count=ROWS):
        self.own, self.held = own, held
        self.start, self.count = start, count
        self.send, self.recv = send, recv
        self.hand_send, self.hand_recv = hand_send, hand_recv
        self.x, self.y, self.z, self.core = place()
        self.dp = self.x * NY + self.y
        self.started = []

    def slot(self, z, core):
        return lax.rem(z + NZ, NZ) * 2 + core

    def part(self, z, core, step, way):
        start, count = self.start, self.count
        if step == NZ // 2:
            count = count // 2
            start = start + way * count
        return self.held.at[self.slot(z, core), pl.ds(start, count)]

    def hop(self, step, way):
        sign = 1 - 2 * way
        origin = self.z - sign * (step - 1)
        target = self.slot(self.z + sign, self.core)
        dst = self.part(origin, self.core, step, way)
        src = self.own if step == 1 and self.own is not None else dst
        return remote(
            src, dst, self.send.at[step - 1, way], self.recv.at[step - 1, way], self.dp, target
        )

    def hand(self, item, view, core):
        src = view if item or self.own is None else self.own
        return remote(
            src if core is None else view,
            view,
            self.hand_send.at[item],
            self.hand_recv.at[item],
            self.dp,
            self.slot(self.z, 1 - self.core),
        )

    def begin(self):
        for way in range(2):
            copy = self.hop(1, way)
            copy.start()
            self.started.append(copy)
        copy = self.hand(0, self.part(self.z, self.core, 1, 0), None)
        copy.start()
        self.started.append(copy)

    def advance(self, step):
        for way in range(2):
            sign = 1 - 2 * way
            view = self.part(self.z - sign * step, self.core, step, way)
            remote(
                view,
                view,
                self.send.at[step - 1, way],
                self.recv.at[step - 1, way],
                self.dp,
                self.slot(self.z + sign, self.core),
            ).wait_recv()
            if step < NZ // 2:
                copy = self.hop(step + 1, way)
                copy.start()
                self.started.append(copy)
            copy = self.hand(1 + 2 * (step - 1) + way, view, None)
            copy.start()
            self.started.append(copy)

    def finish(self):
        other = 1 - self.core
        self.hand(0, self.part(self.z, other, 1, 0), other).wait_recv()
        for step in range(1, NZ // 2 + 1):
            for way in range(2):
                sign = 1 - 2 * way
                view = self.part(self.z - sign * step, other, step, way)
                self.hand(1 + 2 * (step - 1) + way, view, other).wait_recv()
        for copy in self.started:
            copy.wait_send()


GATHER_SEMS = (
    pltpu.SemaphoreType.DMA((NZ // 2, 2)),
    pltpu.SemaphoreType.DMA((NZ // 2, 2)),
    pltpu.SemaphoreType.DMA((NZ + 1,)),
    pltpu.SemaphoreType.DMA((NZ + 1,)),
)


def collect_kernel(
    grad, factor, basis, all_grad, all_factor, all_basis,
    first_right, first_left, sum_right, sum_left,
    right_a, right_b, left_a, left_b, lane_sum, lane_in, half_out,
    own_sem,
    s1, r1, s2, r2, s3, r3, ys, yr, ex_send, ex_recv,
    *gather_sems,
):
    x, y, z, core = place()
    me = z * 2 + core
    side = lax.rem(y, 2)
    dp = x * NY + y
    right = lax.rem(x + 1, NX) * NY + y
    left = lax.rem(x + NX - 1, NX) * NY + y
    partner = x * NY + y + 1 - 2 * side
    peers = [(right, me), (left, me)]
    peers += [(x * NY + lax.rem(y + d, NY), me) for d in range(1, NY)]
    peers += [
        (dp, lax.rem(z + 1, NZ) * 2 + core),
        (dp, lax.rem(z + NZ - 1, NZ) * 2 + core),
        (dp, z * 2 + 1 - core),
    ]
    meet(peers)

    def region(owner, part, chunk):
        owner = lax.rem(owner + NX, NX)
        start = pl.multiple_of(lax.rem(owner, 2) * 4096 + part * 2048, 2048)
        return owner // 2, pl.ds(chunk * CROWS, CROWS), pl.ds(start, 2048)

    started = []

    def begin(copy):
        copy.start()
        started.append(copy)
        return copy

    for r in range(CHUNKS):
        begin(remote(grad.at[region(x + 2, 0, r)], first_right.at[r], s1.at[r, 0], r1.at[r, 0], right, me))
        begin(remote(grad.at[region(x - 2, 1, r)], first_left.at[r], s1.at[r, 1], r1.at[r, 1], left, me))
    own_basis = pltpu.make_async_copy(basis, all_basis.at[me], own_sem)
    own_basis.start()
    all_factor[me] = factor[...].astype(BF16)
    gather_b = Gather(basis, all_basis, *gather_sems[0:4])
    gather_f = Gather(None, all_factor, *gather_sems[4:8])
    gather_g = [
        Gather(None, all_grad, *gather_sems[8 + 4 * h:12 + 4 * h], 2 * h * CROWS, 2 * CROWS) for h in range(2)
    ]
    gather_b.begin()
    gather_f.begin()

    def forward(r):
        remote(first_right.at[r], first_right.at[r], s1.at[r, 0], r1.at[r, 0], right, me).wait_recv()
        own = grad[region(x + 1, 0, r)].astype(F32)
        sum_right[r] = (own + first_right[r].astype(F32)).astype(BF16)
        begin(remote(sum_right.at[r], right_a.at[r], s2.at[r, 0], r2.at[r, 0], right, me))
        begin(remote(grad.at[region(x + 1, 1, r)], right_b.at[r], s3.at[r, 0], r3.at[r, 0], right, me))
        remote(first_left.at[r], first_left.at[r], s1.at[r, 1], r1.at[r, 1], left, me).wait_recv()
        own = grad[region(x - 1, 1, r)].astype(F32)
        sum_left[r] = (own + first_left[r].astype(F32)).astype(BF16)
        begin(remote(sum_left.at[r], left_b.at[r], s2.at[r, 1], r2.at[r, 1], left, me))
        begin(remote(grad.at[region(x - 1, 0, r)], left_a.at[r], s3.at[r, 1], r3.at[r, 1], left, me))

    def turn(r):
        remote(right_a.at[r], right_a.at[r], s2.at[r, 0], r2.at[r, 0], right, me).wait_recv()
        remote(right_b.at[r], right_b.at[r], s3.at[r, 0], r3.at[r, 0], right, me).wait_recv()
        remote(left_b.at[r], left_b.at[r], s2.at[r, 1], r2.at[r, 1], left, me).wait_recv()
        remote(left_a.at[r], left_a.at[r], s3.at[r, 1], r3.at[r, 1], left, me).wait_recv()
        rows = pl.ds(r * CROWS, CROWS)
        for part, (from_left, from_right) in enumerate(((right_a, left_a), (right_b, left_b))):
            total = grad[region(x, part, r)].astype(F32)
            total = total + from_left[r].astype(F32) + from_right[r].astype(F32)
            total = total.astype(BF16)
            for piece in range(4):
                lane_sum[part * 4 + piece, rows] = total[:, piece * HALF:(piece + 1) * HALF]
        if r % 2:
            send_rows = pl.ds((r - 1) * CROWS, 2 * CROWS)
            for d in range(1, NY):
                target = lax.rem(y + d, NY)
                begin(remote(
                    lane_sum.at[target, send_rows], lane_in.at[d - 1, send_rows],
                    ys.at[d - 1, r // 2], yr.at[d - 1, r // 2], x * NY + target, me,
                ))

    mine = pl.ds(pl.multiple_of(side * HALF, HALF), HALF)
    theirs = pl.ds(pl.multiple_of((1 - side) * HALF, HALF), HALF)

    def land(h):
        rows = pl.ds(2 * h * CROWS, 2 * CROWS)
        total = lane_sum[y, rows].astype(F32)
        for d in range(1, NY):
            view = lane_in.at[d - 1, rows]
            remote(view, view, ys.at[d - 1, h], yr.at[d - 1, h], x * NY + lax.rem(y + d, NY), me).wait_recv()
        for d in range(1, NY):
            total = total + lane_in[d - 1, rows].astype(F32)
        total = total.astype(BF16)
        half_out[rows] = total
        all_grad[me, rows, mine] = total
        begin(remote(half_out.at[rows], all_grad.at[me, rows, mine], ex_send.at[h], ex_recv.at[h], partner, me))

    def paired(h):
        view = all_grad.at[me, pl.ds(2 * h * CROWS, 2 * CROWS), theirs]
        remote(view, view, ex_send.at[h], ex_recv.at[h], partner, me).wait_recv()
        gather_g[h].begin()

    forward(0)
    forward(1)
    forward(2)
    gather_b.advance(1)
    forward(3)
    turn(0)
    gather_f.advance(1)
    turn(1)
    turn(2)
    gather_b.advance(2)
    turn(3)
    gather_f.advance(2)
    land(0)
    gather_b.advance(3)
    paired(0)
    land(1)
    gather_g[0].advance(1)
    paired(1)
    gather_f.advance(3)
    gather_g[0].advance(2)
    gather_g[1].advance(1)
    gather_b.advance(4)
    gather_f.advance(4)
    gather_g[0].advance(3)
    gather_g[1].advance(2)
    gather_g[0].advance(4)
    gather_g[1].advance(3)
    gather_g[1].advance(4)
    own_basis.wait()
    gather_b.finish()
    gather_f.finish()
    gather_g[0].finish()
    gather_g[1].finish()
    for copy in started:
        copy.wait_send()


def collect(grad, factor, basis):
    slots = 2 * NZ
    chunk = pltpu.VMEM((CHUNKS, CROWS, 2048), BF16)
    dma = pltpu.SemaphoreType.DMA
    return pl.pallas_call(
        collect_kernel,
        out_shape=(
            jax.ShapeDtypeStruct((slots, ROWS, BLOCK), BF16),
            jax.ShapeDtypeStruct((slots, ROWS, BLOCK), BF16),
            jax.ShapeDtypeStruct((slots, ROWS, BLOCK), F32),
        ),
        in_specs=[VMEM_SPEC] * 3,
        out_specs=(VMEM_SPEC,) * 3,
        scratch_shapes=[chunk] * 8
        + [
            pltpu.VMEM((NY, ROWS, HALF), BF16),
            pltpu.VMEM((NY - 1, ROWS, HALF), BF16),
            pltpu.VMEM((ROWS, HALF), BF16),
            dma(()),
        ]
        + [dma((CHUNKS, 2))] * 6
        + [dma((NY - 1, 2))] * 2
        + [dma((2,))] * 2
        + list(GATHER_SEMS) * 4,
        compiler_params=pltpu.CompilerParams(
            collective_id=0, has_side_effects=True, vmem_limit_bytes=VMEM_BYTES
        ),
        name="collect",
    )(grad, factor, basis)


def split(value):
    high = value.astype(BF16)
    return high, (value - high.astype(F32)).astype(BF16)


def dot3(left, right, numbers):
    dot = functools.partial(lax.dot_general, dimension_numbers=numbers, preferred_element_type=F32)
    return dot(left[0], right[0]) + (dot(left[0], right[1]) + dot(left[1], right[0]))


def factor_inverse(rows):
    count = len(rows)
    shape = rows[0].shape
    lane = lax.broadcasted_iota(jnp.int32, shape, 1)
    sub = lax.broadcasted_iota(jnp.int32, shape, 0)

    def along(value, column):
        return jnp.broadcast_to(value[:, column:column + 1], shape)

    def down(value, row):
        return jnp.broadcast_to(value[row:row + 1], shape)

    rows = list(rows)
    done = []
    columns = [along(rows[0], l) for l in range(8)]
    for group in range(count):
        base = 8 * group
        here = rows[group]
        more = group + 1 < count
        result = jnp.zeros(shape, F32)
        if more:
            below = rows[group + 1]
            below_columns = [along(below, base + l) for l in range(8)]
            next_columns = [along(below, base + 8 + l) for l in range(8)]
        for k in range(8):
            own = sub == k
            pivot = down(columns[k], k)
            inverse = 1.0 / pivot
            row = jnp.where(lane == base + k, 1.0, down(here, k))
            ahead = [down(columns[l], k) for l in range(k + 1, 8)]
            result = jnp.where(own, row * lax.rsqrt(pivot), result)
            scale = jnp.where(own, -inverse, columns[k] * inverse)
            here = jnp.where(own | (lane == base + k), 0.0, here) - scale * row
            for l in range(k + 1, 8):
                columns[l] = jnp.where(own, 0.0, columns[l]) - scale * ahead[l - k - 1]
            if more:
                scale = below_columns[k] * inverse
                below = jnp.where(lane == base + k, 0.0, below) - scale * row
                for l in range(k + 1, 8):
                    below_columns[l] = below_columns[l] - scale * ahead[l - k - 1]
                for l in range(8):
                    next_columns[l] = next_columns[l] - scale * down(below_columns[k], l)
        done.append(jnp.where(lane <= base + sub, result, 0.0))
        if more:
            rows[group + 1] = below
            columns = next_columns
        if group + 2 < count:
            spread = [down(here, l) for l in range(8)]
            inside = (lane >= base) & (lane < base + 8)
            for n in range(group + 2, count):
                terms = [along(rows[n], base + l) * spread[l] for l in range(8)]
                while len(terms) > 1:
                    terms = [terms[i] + terms[i + 1] for i in range(0, len(terms), 2)]
                rows[n] = jnp.where(inside, 0.0, rows[n]) - terms[0]
    return done


def refresh_kernel(
    grad, factor, basis, own_factor, new_factor, basis_t, new_rows,
    power, high, low, gram, upper, lower,
):
    x, y, z, core = place()
    me = z * 2 + core
    side = lax.rem(y, 2)
    tile = 256

    @pl.when(side == 0)
    def _():
        @pl.loop(0, BLOCK // tile)
        def _(i):
            rows = pl.ds(pl.multiple_of(i * tile, tile), tile)
            power[rows, :] = lax.dot_general(grad[rows, :], grad[...], NT, preferred_element_type=F32)

    @pl.when(side == 1)
    def _():
        @pl.loop(0, BLOCK // tile)
        def _(i):
            rows = pl.ds(pl.multiple_of(i * tile, tile), tile)
            power[rows, :] = lax.dot_general(grad[:, rows], grad[...], TN, preferred_element_type=F32)

    mine = pl.ds(pl.multiple_of(me * ROWS, ROWS), ROWS)
    new_factor[...] = 0.95 * own_factor[...] + 0.05 * power[mine, :]

    @pl.loop(0, BLOCK // PANEL)
    def _(i):
        rows = pl.ds(pl.multiple_of(i * PANEL, PANEL), PANEL)
        now = 0.95 * factor[rows, :].astype(F32) + 0.05 * power[rows, :]
        high[rows, :], low[rows, :] = split(now)

    @pl.loop(0, BLOCK // tile)
    def _(i):
        rows = pl.ds(pl.multiple_of(i * tile, tile), tile)
        power[rows, :] = dot3(split(basis[:, rows]), (high[...], low[...]), TN)

    def factored(dst, corner):
        rows = [gram[corner + 8 * i:corner + 8 * i + 8, corner:corner + PANEL] for i in range(PANEL // 8)]
        for i, value in enumerate(factor_inverse(rows)):
            dst[8 * i:8 * i + 8, :] = value
        return split(dst[...])

    top, bottom = slice(0, PANEL), slice(PANEL, 2 * PANEL)

    @pl.loop(0, BLOCK // tile)
    def _(k):
        rows = pl.ds(pl.multiple_of(k * tile, tile), tile)
        panel = split(power[rows, :])
        gram[...] = dot3(panel, panel, NT)
        first = factored(upper, 0)
        below = split(dot3(split(gram[bottom, top]), first, NT))
        gram[bottom, bottom] = gram[bottom, bottom] - dot3(below, below, NT)
        cross = split(dot3(below, first, NN))
        second = factored(lower, PANEL)
        gram[top, top] = upper[...]
        gram[top, bottom] = jnp.zeros((PANEL, PANEL), F32)
        gram[bottom, top] = -dot3(second, cross, NN)
        gram[bottom, bottom] = lower[...]
        fresh = dot3(split(gram[...]), panel, NN)
        basis_t[rows, :] = fresh.astype(BF16)
        fresh = split(fresh)

        @pl.loop(k + 1, BLOCK // tile)
        def _(j):
            later = pl.ds(pl.multiple_of(j * tile, tile), tile)
            old = power[later, :]
            overlap = dot3(split(old), fresh, NT)
            power[later, :] = old - dot3(split(overlap), fresh, NN)

    pick = lax.broadcasted_iota(jnp.int32, (ROWS, BLOCK), 1) == me * ROWS + lax.broadcasted_iota(
        jnp.int32, (ROWS, BLOCK), 0
    )
    new_rows[...] = lax.dot_general(
        pick.astype(BF16), basis_t[...], NT, preferred_element_type=F32
    ).astype(BF16)


def refresh(grad, factor, basis, own_factor):
    return pl.pallas_call(
        refresh_kernel,
        out_shape=(
            jax.ShapeDtypeStruct((ROWS, BLOCK), F32),
            jax.ShapeDtypeStruct((BLOCK, BLOCK), BF16),
            jax.ShapeDtypeStruct((ROWS, BLOCK), BF16),
        ),
        in_specs=[VMEM_SPEC] * 4,
        out_specs=(VMEM_SPEC,) * 3,
        scratch_shapes=[
            pltpu.VMEM((BLOCK, BLOCK), F32),
            pltpu.VMEM((BLOCK, BLOCK), BF16),
            pltpu.VMEM((BLOCK, BLOCK), BF16),
            pltpu.VMEM((2 * PANEL, 2 * PANEL), F32),
            pltpu.VMEM((PANEL, PANEL), F32),
            pltpu.VMEM((PANEL, PANEL), F32),
        ],
        compiler_params=pltpu.CompilerParams(vmem_limit_bytes=VMEM_BYTES),
        name="refresh",
    )(grad, factor, basis, own_factor)


def rotate_kernel(
    basis_t, grad, new_rows, first, second, new_first, new_second, direction,
    mixed, mixed_in, left_rows, part, part_in, all_normal, weighted, weighted_in, turned, turned_in,
    send, recv, *gather_sems,
):
    x, y, z, core = place()
    me = z * 2 + core
    side = lax.rem(y, 2)
    dp = x * NY + y
    partner = dp + 1 - 2 * side
    meet([
        (partner, me),
        (dp, lax.rem(z + 1, NZ) * 2 + core),
        (dp, lax.rem(z + NZ - 1, NZ) * 2 + core),
        (dp, z * 2 + 1 - core),
    ])

    def across(src, dst, i):
        return remote(src, dst, send.at[i], recv.at[i], partner, me)

    def dot(a, b, numbers):
        return lax.dot_general(a, b, numbers, preferred_element_type=F32)

    count = ROWS // 2
    halves = [pl.ds(h * count, count) for h in range(2)]
    to_rows = across(new_rows, left_rows, 0)
    to_mixed = [across(mixed.at[r], mixed_in.at[r], 1 + h) for h, r in enumerate(halves)]
    to_part = [across(part.at[r], part_in.at[r], 3 + h) for h, r in enumerate(halves)]
    to_weighted = [across(weighted.at[r], weighted_in.at[r], 5 + h) for h, r in enumerate(halves)]
    to_turned = [across(turned.at[r], turned_in.at[r], 7 + h) for h, r in enumerate(halves)]
    gathers = [
        Gather(None, all_normal, *gather_sems[4 * h:4 * h + 4], h * count, count) for h in range(2)
    ]
    mine = pl.ds(pl.multiple_of(me * ROWS, ROWS), ROWS)

    @pl.when(side == 0)
    def _():
        mixed[...] = dot(basis_t[mine, :], grad[...], NN).astype(BF16)
        for copy in to_mixed:
            copy.start()
        to_rows.start()
        left_rows[...] = new_rows[...]

    for h, rows in enumerate(halves):
        @pl.when(side == 0)
        def _():
            to_part[h].wait_recv()

        @pl.when(side == 1)
        def _():
            to_mixed[h].wait_recv()
            now = mixed_in[rows, :]
            part[rows, :] = dot(now, basis_t[0:HALF, :], NT)
            to_part[h].start()
            part_in[rows, :] = dot(now, basis_t[HALF:BLOCK, :], NT)

        rotated = part_in[rows, :]
        first_now = 0.95 * first[rows, :] + 0.05 * rotated
        second_now = 0.95 * second[rows, :] + 0.05 * rotated * rotated
        all_normal[me, rows] = (first_now / (jnp.sqrt(second_now) + 1e-08)).astype(BF16)
        gathers[h].begin()
        new_first[rows, :] = first_now
        new_second[rows, :] = second_now

    @pl.when(side == 1)
    def _():
        to_rows.wait_recv()

    for step in range(1, NZ // 2 + 1):
        for gather in gathers:
            gather.advance(step)
    for gather in gathers:
        gather.finish()
    weighted[...] = dot(left_rows[...], all_normal[...].reshape(BLOCK, HALF), NN).astype(BF16)

    @pl.when(side == 0)
    def _():
        for copy in to_weighted:
            copy.start()
        for h, rows in enumerate(halves):
            to_turned[h].wait_recv()
            direction[rows, :] = turned_in[rows, :]
        for copy in [to_rows] + to_mixed + to_weighted:
            copy.wait_send()

    @pl.when(side == 1)
    def _():
        own = dot(weighted[...], basis_t[HALF:BLOCK, :], NN)
        for h, rows in enumerate(halves):
            to_weighted[h].wait_recv()
            total = own[h * count:(h + 1) * count] + dot(weighted_in[rows, :], basis_t[0:HALF, :], NN)
            total = total.astype(BF16)
            turned[rows, :] = total[:, 0:HALF]
            to_turned[h].start()
            direction[rows, :] = total[:, HALF:BLOCK]
        for copy in to_part + to_turned:
            copy.wait_send()


def rotate(basis_t, grad, new_rows, first, second):
    dma = pltpu.SemaphoreType.DMA
    return pl.pallas_call(
        rotate_kernel,
        out_shape=(
            jax.ShapeDtypeStruct((ROWS, HALF), F32),
            jax.ShapeDtypeStruct((ROWS, HALF), F32),
            jax.ShapeDtypeStruct((ROWS, HALF), BF16),
        ),
        in_specs=[VMEM_SPEC] * 5,
        out_specs=(VMEM_SPEC,) * 3,
        scratch_shapes=[
            pltpu.VMEM((ROWS, BLOCK), BF16),
            pltpu.VMEM((ROWS, BLOCK), BF16),
            pltpu.VMEM((ROWS, BLOCK), BF16),
            pltpu.VMEM((ROWS, HALF), F32),
            pltpu.VMEM((ROWS, HALF), F32),
            pltpu.VMEM((2 * NZ, ROWS, HALF), BF16),
            pltpu.VMEM((ROWS, HALF), BF16),
            pltpu.VMEM((ROWS, HALF), BF16),
            pltpu.VMEM((ROWS, HALF), BF16),
            pltpu.VMEM((ROWS, HALF), BF16),
            dma((9,)),
            dma((9,)),
            *GATHER_SEMS,
            *GATHER_SEMS,
        ],
        compiler_params=pltpu.CompilerParams(
            collective_id=1, has_side_effects=True, vmem_limit_bytes=VMEM_BYTES
        ),
        name="rotate",
    )(basis_t, grad, new_rows, first, second)


def finish_kernel(*refs):
    count = len(refs) // 2
    for source, target in zip(refs[:count], refs[count:]):
        target[...] = source[...]


def finish(*arrays):
    return pl.pallas_call(
        finish_kernel,
        out_shape=tuple(jax.ShapeDtypeStruct(a.shape, a.dtype) for a in arrays),
        in_specs=[VMEM_SPEC] * len(arrays),
        out_specs=(VMEM_SPEC,) * len(arrays),
        compiler_params=pltpu.CompilerParams(vmem_limit_bytes=8 << 20),
        name="finish",
    )(*arrays)


def body(grad_partial, factors, bases, first_moment, second_moment):
    all_grad, all_factor, all_basis = collect(grad_partial[0], factors[0], bases[0])
    whole = (BLOCK, BLOCK)
    all_grad = all_grad.reshape(whole)
    new_factor, basis_t, new_rows = refresh(
        all_grad, all_factor.reshape(whole), all_basis.reshape(whole), factors[0]
    )
    first_new, second_new, direction = finish(
        *rotate(basis_t, all_grad, new_rows, first_moment[0], second_moment[0])
    )
    return (new_factor[None], new_rows[None], first_new[None], second_new[None], direction[None])


def solution(mesh):
    spec = P("dp", "fsdp", None)
    return jax.shard_map(
        body,
        mesh=mesh,
        in_specs=(P("dp", None, "fsdp", None), spec, spec, spec, spec),
        out_specs=(spec,) * 5,
        check_vma=False,
    )
```

```python
import functools

import jax
import jax.numpy as jnp
from jax import lax
from jax.experimental import pallas as pl
from jax.experimental.pallas import tpu as pltpu
from jax.sharding import PartitionSpec as P

F32 = jnp.float32
BF16 = jnp.bfloat16
NN = (((1,), (0,)), ((), ()))
NT = (((1,), (1,)), ((), ()))
TN = (((0,), (0,)), ((), ()))
NX, NY, NZ = 4, 8, 8
ROWS = 64
BLOCK = 1024
HALF = 512
CHUNKS = 4
CROWS = ROWS // CHUNKS
PANEL = 128
WINDOW = 5 * PANEL
VMEM_SPEC = pl.BlockSpec(memory_space=pltpu.VMEM)
VMEM_BYTES = 40 << 20


def place():
    dp = lax.axis_index("dp")
    fsdp = lax.axis_index("fsdp")
    return dp // NY, lax.rem(dp, NY), fsdp // 2, lax.rem(fsdp, 2)


def remote(src, dst, send, recv, dp, fsdp):
    return pltpu.make_async_remote_copy(
        src_ref=src,
        dst_ref=dst,
        send_sem=send,
        recv_sem=recv,
        device_id={"dp": dp, "fsdp": fsdp},
        device_id_type=pl.DeviceIdType.MESH,
    )


def meet(peers):
    barrier = pltpu.get_barrier_semaphore()
    for dp, fsdp in peers:
        pl.semaphore_signal(
            barrier,
            inc=1,
            device_id={"dp": dp, "fsdp": fsdp},
            device_id_type=pl.DeviceIdType.MESH,
        )
    pl.semaphore_wait(barrier, len(peers))


class Gather:
    def __init__(self, own, held, send, recv, hand_send, hand_recv, start=0, count=ROWS):
        self.own, self.held = own, held
        self.start, self.count = start, count
        self.send, self.recv = send, recv
        self.hand_send, self.hand_recv = hand_send, hand_recv
        self.x, self.y, self.z, self.core = place()
        self.dp = self.x * NY + self.y
        self.started = []

    def slot(self, z, core):
        return lax.rem(z + NZ, NZ) * 2 + core

    def part(self, z, core, step, way):
        start, count = self.start, self.count
        if step == NZ // 2:
            count = count // 2
            start = start + way * count
        return self.held.at[self.slot(z, core), pl.ds(start, count)]

    def hop(self, step, way):
        sign = 1 - 2 * way
        origin = self.z - sign * (step - 1)
        target = self.slot(self.z + sign, self.core)
        dst = self.part(origin, self.core, step, way)
        src = self.own if step == 1 and self.own is not None else dst
        return remote(
            src, dst, self.send.at[step - 1, way], self.recv.at[step - 1, way], self.dp, target
        )

    def hand(self, item, view, core):
        src = view if item or self.own is None else self.own
        return remote(
            src if core is None else view,
            view,
            self.hand_send.at[item],
            self.hand_recv.at[item],
            self.dp,
            self.slot(self.z, 1 - self.core),
        )

    def begin(self):
        for way in range(2):
            copy = self.hop(1, way)
            copy.start()
            self.started.append(copy)
        copy = self.hand(0, self.part(self.z, self.core, 1, 0), None)
        copy.start()
        self.started.append(copy)

    def advance(self, step):
        for way in range(2):
            sign = 1 - 2 * way
            view = self.part(self.z - sign * step, self.core, step, way)
            remote(
                view,
                view,
                self.send.at[step - 1, way],
                self.recv.at[step - 1, way],
                self.dp,
                self.slot(self.z + sign, self.core),
            ).wait_recv()
            if step < NZ // 2:
                copy = self.hop(step + 1, way)
                copy.start()
                self.started.append(copy)
            copy = self.hand(1 + 2 * (step - 1) + way, view, None)
            copy.start()
            self.started.append(copy)

    def finish(self):
        other = 1 - self.core
        self.hand(0, self.part(self.z, other, 1, 0), other).wait_recv()
        for step in range(1, NZ // 2 + 1):
            for way in range(2):
                sign = 1 - 2 * way
                view = self.part(self.z - sign * step, other, step, way)
                self.hand(1 + 2 * (step - 1) + way, view, other).wait_recv()
        for copy in self.started:
            copy.wait_send()


GATHER_SEMS = (
    pltpu.SemaphoreType.DMA((NZ // 2, 2)),
    pltpu.SemaphoreType.DMA((NZ // 2, 2)),
    pltpu.SemaphoreType.DMA((NZ + 1,)),
    pltpu.SemaphoreType.DMA((NZ + 1,)),
)


def collect_kernel(
    grad_hbm, factor_hbm, basis_hbm, all_grad, all_factor, all_basis,
    grad, factor, basis, first_right, first_left, sum_right, sum_left,
    right_a, right_b, left_a, left_b, lane_sum, lane_in, half_out,
    own_sem,
    s1, r1, s2, r2, s3, r3, ys, yr, ex_send, ex_recv,
    *gather_sems,
):
    x, y, z, core = place()
    me = z * 2 + core
    side = lax.rem(y, 2)
    dp = x * NY + y
    right = lax.rem(x + 1, NX) * NY + y
    left = lax.rem(x + NX - 1, NX) * NY + y
    partner = x * NY + y + 1 - 2 * side
    peers = [(right, me), (left, me)]
    peers += [(x * NY + lax.rem(y + d, NY), me) for d in range(1, NY)]
    peers += [
        (dp, lax.rem(z + 1, NZ) * 2 + core),
        (dp, lax.rem(z + NZ - 1, NZ) * 2 + core),
        (dp, z * 2 + 1 - core),
    ]
    staged = [
        pltpu.make_async_copy(src, dst, own_sem.at[i])
        for i, (src, dst) in enumerate(((grad_hbm, grad), (basis_hbm, basis), (factor_hbm, factor)))
    ]
    for copy in staged:
        copy.start()
    meet(peers)
    staged[0].wait()

    def region(owner, part, chunk):
        owner = lax.rem(owner + NX, NX)
        start = pl.multiple_of(lax.rem(owner, 2) * 4096 + part * 2048, 2048)
        return owner // 2, pl.ds(chunk * CROWS, CROWS), pl.ds(start, 2048)

    started = []

    def begin(copy):
        copy.start()
        started.append(copy)
        return copy

    for r in range(CHUNKS):
        begin(remote(grad.at[region(x + 2, 0, r)], first_right.at[r], s1.at[r, 0], r1.at[r, 0], right, me))
        begin(remote(grad.at[region(x - 2, 1, r)], first_left.at[r], s1.at[r, 1], r1.at[r, 1], left, me))
    gather_b = Gather(None, all_basis, *gather_sems[0:4])
    gather_f = Gather(None, all_factor, *gather_sems[4:8])
    gather_g = [
        Gather(None, all_grad, *gather_sems[8 + 4 * h:12 + 4 * h], 2 * h * CROWS, 2 * CROWS) for h in range(2)
    ]
    staged[1].wait()
    all_basis[me] = basis[...].astype(BF16)
    gather_b.begin()
    staged[2].wait()
    for block in range(WINDOW // PANEL):
        start = pl.multiple_of(lax.rem(z + block, NZ) * PANEL, PANEL)
        all_factor[me, :, block * PANEL:(block + 1) * PANEL] = factor[:, pl.ds(start, PANEL)]
    gather_f.begin()

    def forward(r):
        remote(first_right.at[r], first_right.at[r], s1.at[r, 0], r1.at[r, 0], right, me).wait_recv()
        own = grad[region(x + 1, 0, r)].astype(F32)
        sum_right[r] = (own + first_right[r].astype(F32)).astype(BF16)
        begin(remote(sum_right.at[r], right_a.at[r], s2.at[r, 0], r2.at[r, 0], right, me))
        begin(remote(grad.at[region(x + 1, 1, r)], right_b.at[r], s3.at[r, 0], r3.at[r, 0], right, me))
        remote(first_left.at[r], first_left.at[r], s1.at[r, 1], r1.at[r, 1], left, me).wait_recv()
        own = grad[region(x - 1, 1, r)].astype(F32)
        sum_left[r] = (own + first_left[r].astype(F32)).astype(BF16)
        begin(remote(sum_left.at[r], left_b.at[r], s2.at[r, 1], r2.at[r, 1], left, me))
        begin(remote(grad.at[region(x - 1, 0, r)], left_a.at[r], s3.at[r, 1], r3.at[r, 1], left, me))

    def turn(r):
        remote(right_a.at[r], right_a.at[r], s2.at[r, 0], r2.at[r, 0], right, me).wait_recv()
        remote(right_b.at[r], right_b.at[r], s3.at[r, 0], r3.at[r, 0], right, me).wait_recv()
        remote(left_b.at[r], left_b.at[r], s2.at[r, 1], r2.at[r, 1], left, me).wait_recv()
        remote(left_a.at[r], left_a.at[r], s3.at[r, 1], r3.at[r, 1], left, me).wait_recv()
        rows = pl.ds(r * CROWS, CROWS)
        for part, (from_left, from_right) in enumerate(((right_a, left_a), (right_b, left_b))):
            total = grad[region(x, part, r)].astype(F32)
            total = total + from_left[r].astype(F32) + from_right[r].astype(F32)
            total = total.astype(BF16)
            for piece in range(4):
                lane_sum[part * 4 + piece, rows] = total[:, piece * HALF:(piece + 1) * HALF]
        if r % 2:
            send_rows = pl.ds((r - 1) * CROWS, 2 * CROWS)
            for d in range(1, NY):
                target = lax.rem(y + d, NY)
                begin(remote(
                    lane_sum.at[target, send_rows], lane_in.at[d - 1, send_rows],
                    ys.at[d - 1, r // 2], yr.at[d - 1, r // 2], x * NY + target, me,
                ))

    mine = pl.ds(pl.multiple_of(side * HALF, HALF), HALF)
    theirs = pl.ds(pl.multiple_of((1 - side) * HALF, HALF), HALF)

    def land(h):
        rows = pl.ds(2 * h * CROWS, 2 * CROWS)
        total = lane_sum[y, rows].astype(F32)
        for d in range(1, NY):
            view = lane_in.at[d - 1, rows]
            remote(view, view, ys.at[d - 1, h], yr.at[d - 1, h], x * NY + lax.rem(y + d, NY), me).wait_recv()
        for d in range(1, NY):
            total = total + lane_in[d - 1, rows].astype(F32)
        total = total.astype(BF16)
        half_out[rows] = total
        all_grad[me, rows, mine] = total
        begin(remote(half_out.at[rows], all_grad.at[me, rows, mine], ex_send.at[h], ex_recv.at[h], partner, me))

    def paired(h):
        view = all_grad.at[me, pl.ds(2 * h * CROWS, 2 * CROWS), theirs]
        remote(view, view, ex_send.at[h], ex_recv.at[h], partner, me).wait_recv()
        gather_g[h].begin()

    forward(0)
    forward(1)
    gather_b.advance(1)
    forward(2)
    forward(3)
    gather_f.advance(1)
    turn(0)
    gather_b.advance(2)
    turn(1)
    gather_f.advance(2)
    turn(2)
    gather_b.advance(3)
    turn(3)
    gather_f.advance(3)
    land(0)
    gather_b.advance(4)
    paired(0)
    gather_f.advance(4)
    gather_g[0].advance(1)
    land(1)
    gather_g[0].advance(2)
    paired(1)
    gather_g[0].advance(3)
    gather_g[1].advance(1)
    gather_g[0].advance(4)
    gather_g[1].advance(2)
    gather_g[1].advance(3)
    gather_g[1].advance(4)
    gather_b.finish()
    gather_f.finish()
    gather_g[0].finish()
    gather_g[1].finish()
    for copy in started:
        copy.wait_send()


def collect(grad, factor, basis):
    slots = 2 * NZ
    chunk = pltpu.VMEM((CHUNKS, CROWS, 2048), BF16)
    dma = pltpu.SemaphoreType.DMA
    return pl.pallas_call(
        collect_kernel,
        out_shape=(
            jax.ShapeDtypeStruct((slots, ROWS, BLOCK), BF16),
            jax.ShapeDtypeStruct((slots, ROWS, WINDOW), F32),
            jax.ShapeDtypeStruct((slots, ROWS, BLOCK), BF16),
        ),
        in_specs=[pl.BlockSpec(memory_space=pltpu.HBM)] * 3,
        out_specs=(VMEM_SPEC,) * 3,
        scratch_shapes=[
            pltpu.VMEM(grad.shape, BF16),
            pltpu.VMEM(factor.shape, F32),
            pltpu.VMEM(basis.shape, F32),
        ]
        + [chunk] * 8
        + [
            pltpu.VMEM((NY, ROWS, HALF), BF16),
            pltpu.VMEM((NY - 1, ROWS, HALF), BF16),
            pltpu.VMEM((ROWS, HALF), BF16),
            dma((3,)),
        ]
        + [dma((CHUNKS, 2))] * 6
        + [dma((NY - 1, 2))] * 2
        + [dma((2,))] * 2
        + list(GATHER_SEMS) * 4,
        compiler_params=pltpu.CompilerParams(
            collective_id=0, has_side_effects=True, vmem_limit_bytes=VMEM_BYTES
        ),
        name="collect",
    )(*(pltpu.with_memory_space_constraint(a, pltpu.HBM) for a in (grad, factor, basis)))


def split(value):
    high = value.astype(BF16)
    return high, (value - high.astype(F32)).astype(BF16)


def dot3(left, right, numbers):
    dot = functools.partial(lax.dot_general, dimension_numbers=numbers, preferred_element_type=F32)
    return dot(left[0], right[0]) + (dot(left[0], right[1]) + dot(left[1], right[0]))


def factor_inverse(rows):
    count = len(rows)
    shape = rows[0].shape
    lane = lax.broadcasted_iota(jnp.int32, shape, 1)
    sub = lax.broadcasted_iota(jnp.int32, shape, 0)

    def along(value, column):
        return jnp.broadcast_to(value[:, column:column + 1], shape)

    def down(value, row):
        return jnp.broadcast_to(value[row:row + 1], shape)

    rows = list(rows)
    done = []
    columns = [along(rows[0], l) for l in range(8)]
    for group in range(count):
        base = 8 * group
        here = rows[group]
        more = group + 1 < count
        result = jnp.zeros(shape, F32)
        if more:
            below = rows[group + 1]
            below_columns = [along(below, base + l) for l in range(8)]
            next_columns = [along(below, base + 8 + l) for l in range(8)]
        for k in range(8):
            own = sub == k
            pivot = down(columns[k], k)
            inverse = 1.0 / pivot
            row = jnp.where(lane == base + k, 1.0, down(here, k))
            ahead = [down(columns[l], k) for l in range(k + 1, 8)]
            result = jnp.where(own, row * lax.rsqrt(pivot), result)
            scale = jnp.where(own, -inverse, columns[k] * inverse)
            here = jnp.where(own | (lane == base + k), 0.0, here) - scale * row
            for l in range(k + 1, 8):
                columns[l] = jnp.where(own, 0.0, columns[l]) - scale * ahead[l - k - 1]
            if more:
                scale = below_columns[k] * inverse
                below = jnp.where(lane == base + k, 0.0, below) - scale * row
                for l in range(k + 1, 8):
                    below_columns[l] = below_columns[l] - scale * ahead[l - k - 1]
                for l in range(8):
                    next_columns[l] = next_columns[l] - scale * down(below_columns[k], l)
        done.append(jnp.where(lane <= base + sub, result, 0.0))
        if more:
            rows[group + 1] = below
            columns = next_columns
        if group + 2 < count:
            spread = [down(here, l) for l in range(8)]
            inside = (lane >= base) & (lane < base + 8)
            for n in range(group + 2, count):
                terms = [along(rows[n], base + l) * spread[l] for l in range(8)]
                while len(terms) > 1:
                    terms = [terms[i] + terms[i + 1] for i in range(0, len(terms), 2)]
                rows[n] = jnp.where(inside, 0.0, rows[n]) - terms[0]
    return done


def refresh_kernel(
    grad, factor, basis, own_factor, new_factor, basis_t, new_rows,
    power, high, low, gram, upper, lower,
):
    x, y, z, core = place()
    me = z * 2 + core
    side = lax.rem(y, 2)
    tile = 256

    @pl.when(side == 0)
    def _():
        @pl.loop(0, BLOCK // tile)
        def _(i):
            rows = pl.ds(pl.multiple_of(i * tile, tile), tile)
            power[rows, :] = lax.dot_general(grad[rows, :], grad[...], NT, preferred_element_type=F32)

    @pl.when(side == 1)
    def _():
        @pl.loop(0, BLOCK // tile)
        def _(i):
            rows = pl.ds(pl.multiple_of(i * tile, tile), tile)
            power[rows, :] = lax.dot_general(grad[:, rows], grad[...], TN, preferred_element_type=F32)

    mine = pl.ds(pl.multiple_of(me * ROWS, ROWS), ROWS)
    new_factor[...] = 0.95 * own_factor[...] + 0.05 * power[mine, :]

    @pl.loop(0, NZ)
    def _(i):
        rows = pl.ds(pl.multiple_of(i * PANEL, PANEL), PANEL)
        for block in range(WINDOW // PANEL):
            columns = pl.ds(pl.multiple_of(lax.rem(i + block, NZ) * PANEL, PANEL), PANEL)
            now = 0.95 * factor[rows, block * PANEL:(block + 1) * PANEL] + 0.05 * power[rows, columns]
            high[rows, columns], low[rows, columns] = split(now)
            if 0 < block < NZ // 2:
                high[columns, rows], low[columns, rows] = split(now.T)

    @pl.loop(0, BLOCK // tile)
    def _(i):
        rows = pl.ds(pl.multiple_of(i * tile, tile), tile)
        now = basis[:, rows]
        power[rows, :] = lax.dot_general(
            now, high[...], TN, preferred_element_type=F32
        ) + lax.dot_general(now, low[...], TN, preferred_element_type=F32)

    def factored(dst, corner):
        rows = [gram[corner + 8 * i:corner + 8 * i + 8, corner:corner + PANEL] for i in range(PANEL // 8)]
        for i, value in enumerate(factor_inverse(rows)):
            dst[8 * i:8 * i + 8, :] = value
        return split(dst[...])

    top, bottom = slice(0, PANEL), slice(PANEL, 2 * PANEL)

    @pl.loop(0, BLOCK // tile)
    def _(k):
        rows = pl.ds(pl.multiple_of(k * tile, tile), tile)
        panel = split(power[rows, :])
        gram[...] = dot3(panel, panel, NT)
        first = factored(upper, 0)
        below = split(dot3(split(gram[bottom, top]), first, NT))
        gram[bottom, bottom] = gram[bottom, bottom] - dot3(below, below, NT)
        cross = split(dot3(below, first, NN))
        second = factored(lower, PANEL)
        gram[top, top] = upper[...]
        gram[top, bottom] = jnp.zeros((PANEL, PANEL), F32)
        gram[bottom, top] = -dot3(second, cross, NN)
        gram[bottom, bottom] = lower[...]
        fresh = dot3(split(gram[...]), panel, NN)
        basis_t[rows, :] = fresh.astype(BF16)
        fresh = split(fresh)

        @pl.loop(k + 1, BLOCK // tile)
        def _(j):
            later = pl.ds(pl.multiple_of(j * tile, tile), tile)
            old = power[later, :]
            overlap = dot3(split(old), fresh, NT)
            power[later, :] = old - dot3(split(overlap), fresh, NN)

    pick = lax.broadcasted_iota(jnp.int32, (ROWS, BLOCK), 1) == me * ROWS + lax.broadcasted_iota(
        jnp.int32, (ROWS, BLOCK), 0
    )
    new_rows[...] = lax.dot_general(
        pick.astype(BF16), basis_t[...], NT, preferred_element_type=F32
    ).astype(BF16)


def refresh(grad, factor, basis, own_factor):
    return pl.pallas_call(
        refresh_kernel,
        out_shape=(
            jax.ShapeDtypeStruct((ROWS, BLOCK), F32),
            jax.ShapeDtypeStruct((BLOCK, BLOCK), BF16),
            jax.ShapeDtypeStruct((ROWS, BLOCK), BF16),
        ),
        in_specs=[VMEM_SPEC] * 4,
        out_specs=(VMEM_SPEC,) * 3,
        scratch_shapes=[
            pltpu.VMEM((BLOCK, BLOCK), F32),
            pltpu.VMEM((BLOCK, BLOCK), BF16),
            pltpu.VMEM((BLOCK, BLOCK), BF16),
            pltpu.VMEM((2 * PANEL, 2 * PANEL), F32),
            pltpu.VMEM((PANEL, PANEL), F32),
            pltpu.VMEM((PANEL, PANEL), F32),
        ],
        compiler_params=pltpu.CompilerParams(vmem_limit_bytes=VMEM_BYTES),
        name="refresh",
    )(grad, factor, basis, own_factor)


def rotate_kernel(
    basis_t, grad, new_rows, first, second, new_first, new_second, direction,
    mixed, mixed_in, left_rows, part, part_in, all_normal, weighted, weighted_in, turned, turned_in,
    send, recv, *gather_sems,
):
    x, y, z, core = place()
    me = z * 2 + core
    side = lax.rem(y, 2)
    dp = x * NY + y
    partner = dp + 1 - 2 * side
    meet([
        (partner, me),
        (dp, lax.rem(z + 1, NZ) * 2 + core),
        (dp, lax.rem(z + NZ - 1, NZ) * 2 + core),
        (dp, z * 2 + 1 - core),
    ])

    def across(src, dst, i):
        return remote(src, dst, send.at[i], recv.at[i], partner, me)

    def dot(a, b, numbers):
        return lax.dot_general(a, b, numbers, preferred_element_type=F32)

    count = ROWS // 2
    halves = [pl.ds(h * count, count) for h in range(2)]
    to_rows = across(new_rows, left_rows, 0)
    to_mixed = [across(mixed.at[r], mixed_in.at[r], 1 + h) for h, r in enumerate(halves)]
    to_part = [across(part.at[r], part_in.at[r], 3 + h) for h, r in enumerate(halves)]
    to_weighted = [across(weighted.at[r], weighted_in.at[r], 5 + h) for h, r in enumerate(halves)]
    to_turned = [across(turned.at[r], turned_in.at[r], 7 + h) for h, r in enumerate(halves)]
    gathers = [
        Gather(None, all_normal, *gather_sems[4 * h:4 * h + 4], h * count, count) for h in range(2)
    ]
    mine = pl.ds(pl.multiple_of(me * ROWS, ROWS), ROWS)

    @pl.when(side == 0)
    def _():
        mixed[...] = dot(basis_t[mine, :], grad[...], NN).astype(BF16)
        for copy in to_mixed:
            copy.start()
        to_rows.start()
        left_rows[...] = new_rows[...]

    for h, rows in enumerate(halves):
        @pl.when(side == 0)
        def _():
            to_part[h].wait_recv()

        @pl.when(side == 1)
        def _():
            to_mixed[h].wait_recv()
            now = mixed_in[rows, :]
            part[rows, :] = dot(now, basis_t[0:HALF, :], NT)
            to_part[h].start()
            part_in[rows, :] = dot(now, basis_t[HALF:BLOCK, :], NT)

        rotated = part_in[rows, :]
        first_now = 0.95 * first[rows, :] + 0.05 * rotated
        second_now = 0.95 * second[rows, :] + 0.05 * rotated * rotated
        all_normal[me, rows] = (first_now / (jnp.sqrt(second_now) + 1e-08)).astype(BF16)
        gathers[h].begin()
        new_first[rows, :] = first_now
        new_second[rows, :] = second_now

    @pl.when(side == 1)
    def _():
        to_rows.wait_recv()

    for step in range(1, NZ // 2 + 1):
        for gather in gathers:
            gather.advance(step)
    for gather in gathers:
        gather.finish()
    weighted[...] = dot(left_rows[...], all_normal[...].reshape(BLOCK, HALF), NN).astype(BF16)

    @pl.when(side == 0)
    def _():
        for copy in to_weighted:
            copy.start()
        for h, rows in enumerate(halves):
            to_turned[h].wait_recv()
            direction[rows, :] = turned_in[rows, :]
        for copy in [to_rows] + to_mixed + to_weighted:
            copy.wait_send()

    @pl.when(side == 1)
    def _():
        own = dot(weighted[...], basis_t[HALF:BLOCK, :], NN)
        for h, rows in enumerate(halves):
            to_weighted[h].wait_recv()
            total = own[h * count:(h + 1) * count] + dot(weighted_in[rows, :], basis_t[0:HALF, :], NN)
            total = total.astype(BF16)
            turned[rows, :] = total[:, 0:HALF]
            to_turned[h].start()
            direction[rows, :] = total[:, HALF:BLOCK]
        for copy in to_part + to_turned:
            copy.wait_send()


def rotate(basis_t, grad, new_rows, first, second):
    dma = pltpu.SemaphoreType.DMA
    return pl.pallas_call(
        rotate_kernel,
        out_shape=(
            jax.ShapeDtypeStruct((ROWS, HALF), F32),
            jax.ShapeDtypeStruct((ROWS, HALF), F32),
            jax.ShapeDtypeStruct((ROWS, HALF), BF16),
        ),
        in_specs=[VMEM_SPEC] * 5,
        out_specs=(VMEM_SPEC,) * 3,
        scratch_shapes=[
            pltpu.VMEM((ROWS, BLOCK), BF16),
            pltpu.VMEM((ROWS, BLOCK), BF16),
            pltpu.VMEM((ROWS, BLOCK), BF16),
            pltpu.VMEM((ROWS, HALF), F32),
            pltpu.VMEM((ROWS, HALF), F32),
            pltpu.VMEM((2 * NZ, ROWS, HALF), BF16),
            pltpu.VMEM((ROWS, HALF), BF16),
            pltpu.VMEM((ROWS, HALF), BF16),
            pltpu.VMEM((ROWS, HALF), BF16),
            pltpu.VMEM((ROWS, HALF), BF16),
            dma((9,)),
            dma((9,)),
            *GATHER_SEMS,
            *GATHER_SEMS,
        ],
        compiler_params=pltpu.CompilerParams(
            collective_id=1, has_side_effects=True, vmem_limit_bytes=VMEM_BYTES
        ),
        name="rotate",
    )(basis_t, grad, new_rows, first, second)


def finish_kernel(*refs):
    count = len(refs) // 2
    for source, target in zip(refs[:count], refs[count:]):
        target[...] = source[...]


def finish(*arrays):
    return pl.pallas_call(
        finish_kernel,
        out_shape=tuple(jax.ShapeDtypeStruct(a.shape, a.dtype) for a in arrays),
        in_specs=[VMEM_SPEC] * len(arrays),
        out_specs=(VMEM_SPEC,) * len(arrays),
        compiler_params=pltpu.CompilerParams(vmem_limit_bytes=8 << 20),
        name="finish",
    )(*arrays)


def body(grad_partial, factors, bases, first_moment, second_moment):
    all_grad, all_factor, all_basis = collect(grad_partial[0], factors[0], bases[0])
    whole = (BLOCK, BLOCK)
    all_grad = all_grad.reshape(whole)
    new_factor, basis_t, new_rows = refresh(
        all_grad, all_factor.reshape(BLOCK, WINDOW), all_basis.reshape(whole), factors[0]
    )
    first_new, second_new, direction, new_rows = finish(
        *rotate(basis_t, all_grad, new_rows, first_moment[0], second_moment[0]), new_rows
    )
    return (new_factor[None], new_rows[None], first_new[None], second_new[None], direction[None])


def solution(mesh):
    spec = P("dp", "fsdp", None)
    return jax.shard_map(
        body,
        mesh=mesh,
        in_specs=(P("dp", None, "fsdp", None), spec, spec, spec, spec),
        out_specs=(spec,) * 5,
        check_vma=False,
    )
```

```python
import functools

import jax
import jax.numpy as jnp
from jax import lax
from jax.experimental import pallas as pl
from jax.experimental.pallas import tpu as pltpu
from jax.sharding import PartitionSpec as P

F32 = jnp.float32
BF16 = jnp.bfloat16
NN = (((1,), (0,)), ((), ()))
NT = (((1,), (1,)), ((), ()))
TN = (((0,), (0,)), ((), ()))
NX, NY, NZ = 4, 8, 8
ROWS = 64
BLOCK = 1024
HALF = 512
CHUNKS = 4
CROWS = ROWS // CHUNKS
PANEL = 128
WINDOW = 5 * PANEL
VMEM_SPEC = pl.BlockSpec(memory_space=pltpu.VMEM)
VMEM_BYTES = 40 << 20


def place():
    dp = lax.axis_index("dp")
    fsdp = lax.axis_index("fsdp")
    return dp // NY, lax.rem(dp, NY), fsdp // 2, lax.rem(fsdp, 2)


def remote(src, dst, send, recv, dp, fsdp):
    return pltpu.make_async_remote_copy(
        src_ref=src,
        dst_ref=dst,
        send_sem=send,
        recv_sem=recv,
        device_id={"dp": dp, "fsdp": fsdp},
        device_id_type=pl.DeviceIdType.MESH,
    )


def greet(peers):
    barrier = pltpu.get_barrier_semaphore()
    for dp, fsdp in peers:
        pl.semaphore_signal(
            barrier,
            inc=1,
            device_id={"dp": dp, "fsdp": fsdp},
            device_id_type=pl.DeviceIdType.MESH,
        )
    return lambda: pl.semaphore_wait(barrier, len(peers))


def meet(peers):
    greet(peers)()


class Gather:
    def __init__(self, own, held, send, recv, hand_send, hand_recv, start=0, count=ROWS):
        self.own, self.held = own, held
        self.start, self.count = start, count
        self.send, self.recv = send, recv
        self.hand_send, self.hand_recv = hand_send, hand_recv
        self.x, self.y, self.z, self.core = place()
        self.dp = self.x * NY + self.y
        self.started = []

    def slot(self, z, core):
        return lax.rem(z + NZ, NZ) * 2 + core

    def part(self, z, core, step, way):
        start, count = self.start, self.count
        if step == NZ // 2:
            count = count // 2
            start = start + way * count
        return self.held.at[self.slot(z, core), pl.ds(start, count)]

    def hop(self, step, way):
        sign = 1 - 2 * way
        origin = self.z - sign * (step - 1)
        target = self.slot(self.z + sign, self.core)
        dst = self.part(origin, self.core, step, way)
        src = self.own if step == 1 and self.own is not None else dst
        return remote(
            src, dst, self.send.at[step - 1, way], self.recv.at[step - 1, way], self.dp, target
        )

    def hand(self, item, view, core):
        src = view if item or self.own is None else self.own
        return remote(
            src if core is None else view,
            view,
            self.hand_send.at[item],
            self.hand_recv.at[item],
            self.dp,
            self.slot(self.z, 1 - self.core),
        )

    def begin(self):
        for way in range(2):
            copy = self.hop(1, way)
            copy.start()
            self.started.append(copy)
        copy = self.hand(0, self.part(self.z, self.core, 1, 0), None)
        copy.start()
        self.started.append(copy)

    def advance(self, step):
        for way in range(2):
            sign = 1 - 2 * way
            view = self.part(self.z - sign * step, self.core, step, way)
            remote(
                view,
                view,
                self.send.at[step - 1, way],
                self.recv.at[step - 1, way],
                self.dp,
                self.slot(self.z + sign, self.core),
            ).wait_recv()
            if step < NZ // 2:
                copy = self.hop(step + 1, way)
                copy.start()
                self.started.append(copy)
            copy = self.hand(1 + 2 * (step - 1) + way, view, None)
            copy.start()
            self.started.append(copy)

    def finish(self):
        other = 1 - self.core
        self.hand(0, self.part(self.z, other, 1, 0), other).wait_recv()
        for step in range(1, NZ // 2 + 1):
            for way in range(2):
                sign = 1 - 2 * way
                view = self.part(self.z - sign * step, other, step, way)
                self.hand(1 + 2 * (step - 1) + way, view, other).wait_recv()
        for copy in self.started:
            copy.wait_send()


GATHER_SEMS = (
    pltpu.SemaphoreType.DMA((NZ // 2, 2)),
    pltpu.SemaphoreType.DMA((NZ // 2, 2)),
    pltpu.SemaphoreType.DMA((NZ + 1,)),
    pltpu.SemaphoreType.DMA((NZ + 1,)),
)


def collect_kernel(
    grad_hbm, factor_hbm, basis_hbm, all_grad, all_factor, all_basis,
    grad, factor, basis, first_right, first_left, sum_right, sum_left,
    right_a, right_b, left_a, left_b, lane_sum, lane_in, half_out,
    own_sem,
    s1, r1, s2, r2, s3, r3, ys, yr, ex_send, ex_recv,
    *gather_sems,
):
    x, y, z, core = place()
    me = z * 2 + core
    side = lax.rem(y, 2)
    dp = x * NY + y
    right = lax.rem(x + 1, NX) * NY + y
    left = lax.rem(x + NX - 1, NX) * NY + y
    partner = x * NY + y + 1 - 2 * side
    peers = [(right, me), (left, me)]
    peers += [(x * NY + lax.rem(y + d, NY), me) for d in range(1, NY)]
    peers += [
        (dp, lax.rem(z + 1, NZ) * 2 + core),
        (dp, lax.rem(z + NZ - 1, NZ) * 2 + core),
        (dp, z * 2 + 1 - core),
    ]
    staged = [
        pltpu.make_async_copy(src, dst, own_sem.at[i])
        for i, (src, dst) in enumerate(((grad_hbm, grad), (basis_hbm, basis), (factor_hbm, factor)))
    ]
    for copy in staged:
        copy.start()
    meet(peers)
    staged[0].wait()

    def region(owner, part, chunk):
        owner = lax.rem(owner + NX, NX)
        start = pl.multiple_of(lax.rem(owner, 2) * 4096 + part * 2048, 2048)
        return owner // 2, pl.ds(chunk * CROWS, CROWS), pl.ds(start, 2048)

    started = []

    def begin(copy):
        copy.start()
        started.append(copy)
        return copy

    for r in range(CHUNKS):
        begin(remote(grad.at[region(x + 2, 0, r)], first_right.at[r], s1.at[r, 0], r1.at[r, 0], right, me))
        begin(remote(grad.at[region(x - 2, 1, r)], first_left.at[r], s1.at[r, 1], r1.at[r, 1], left, me))
    gather_b = Gather(None, all_basis, *gather_sems[0:4])
    gather_f = Gather(None, all_factor, *gather_sems[4:8])
    gather_g = [
        Gather(None, all_grad, *gather_sems[8 + 4 * h:12 + 4 * h], 2 * h * CROWS, 2 * CROWS) for h in range(2)
    ]
    staged[1].wait()
    all_basis[me] = basis[...].astype(BF16)
    gather_b.begin()
    staged[2].wait()
    for block in range(WINDOW // PANEL):
        start = pl.multiple_of(lax.rem(z + block, NZ) * PANEL, PANEL)
        all_factor[me, :, block * PANEL:(block + 1) * PANEL] = factor[:, pl.ds(start, PANEL)]
    gather_f.begin()

    def forward(r):
        remote(first_right.at[r], first_right.at[r], s1.at[r, 0], r1.at[r, 0], right, me).wait_recv()
        own = grad[region(x + 1, 0, r)].astype(F32)
        sum_right[r] = (own + first_right[r].astype(F32)).astype(BF16)
        begin(remote(sum_right.at[r], right_a.at[r], s2.at[r, 0], r2.at[r, 0], right, me))
        begin(remote(grad.at[region(x + 1, 1, r)], right_b.at[r], s3.at[r, 0], r3.at[r, 0], right, me))
        remote(first_left.at[r], first_left.at[r], s1.at[r, 1], r1.at[r, 1], left, me).wait_recv()
        own = grad[region(x - 1, 1, r)].astype(F32)
        sum_left[r] = (own + first_left[r].astype(F32)).astype(BF16)
        begin(remote(sum_left.at[r], left_b.at[r], s2.at[r, 1], r2.at[r, 1], left, me))
        begin(remote(grad.at[region(x - 1, 0, r)], left_a.at[r], s3.at[r, 1], r3.at[r, 1], left, me))

    def turn(r):
        remote(right_a.at[r], right_a.at[r], s2.at[r, 0], r2.at[r, 0], right, me).wait_recv()
        remote(right_b.at[r], right_b.at[r], s3.at[r, 0], r3.at[r, 0], right, me).wait_recv()
        remote(left_b.at[r], left_b.at[r], s2.at[r, 1], r2.at[r, 1], left, me).wait_recv()
        remote(left_a.at[r], left_a.at[r], s3.at[r, 1], r3.at[r, 1], left, me).wait_recv()
        rows = pl.ds(r * CROWS, CROWS)
        for part, (from_left, from_right) in enumerate(((right_a, left_a), (right_b, left_b))):
            total = grad[region(x, part, r)].astype(F32)
            total = total + from_left[r].astype(F32) + from_right[r].astype(F32)
            total = total.astype(BF16)
            for piece in range(4):
                lane_sum[part * 4 + piece, rows] = total[:, piece * HALF:(piece + 1) * HALF]
        if r % 2:
            send_rows = pl.ds((r - 1) * CROWS, 2 * CROWS)
            for d in range(1, NY):
                target = lax.rem(y + d, NY)
                begin(remote(
                    lane_sum.at[target, send_rows], lane_in.at[d - 1, send_rows],
                    ys.at[d - 1, r // 2], yr.at[d - 1, r // 2], x * NY + target, me,
                ))

    mine = pl.ds(pl.multiple_of(side * HALF, HALF), HALF)
    theirs = pl.ds(pl.multiple_of((1 - side) * HALF, HALF), HALF)

    def land(h):
        rows = pl.ds(2 * h * CROWS, 2 * CROWS)
        total = lane_sum[y, rows].astype(F32)
        for d in range(1, NY):
            view = lane_in.at[d - 1, rows]
            remote(view, view, ys.at[d - 1, h], yr.at[d - 1, h], x * NY + lax.rem(y + d, NY), me).wait_recv()
        for d in range(1, NY):
            total = total + lane_in[d - 1, rows].astype(F32)
        total = total.astype(BF16)
        half_out[rows] = total
        all_grad[me, rows, mine] = total
        begin(remote(half_out.at[rows], all_grad.at[me, rows, mine], ex_send.at[h], ex_recv.at[h], partner, me))

    def paired(h):
        view = all_grad.at[me, pl.ds(2 * h * CROWS, 2 * CROWS), theirs]
        remote(view, view, ex_send.at[h], ex_recv.at[h], partner, me).wait_recv()
        gather_g[h].begin()

    forward(0)
    forward(1)
    gather_b.advance(1)
    forward(2)
    forward(3)
    gather_f.advance(1)
    turn(0)
    gather_b.advance(2)
    turn(1)
    gather_f.advance(2)
    turn(2)
    gather_b.advance(3)
    turn(3)
    gather_f.advance(3)
    land(0)
    gather_b.advance(4)
    paired(0)
    gather_f.advance(4)
    gather_g[0].advance(1)
    land(1)
    gather_g[0].advance(2)
    paired(1)
    gather_g[0].advance(3)
    gather_g[1].advance(1)
    gather_g[0].advance(4)
    gather_g[1].advance(2)
    gather_g[1].advance(3)
    gather_g[1].advance(4)
    gather_b.finish()
    gather_f.finish()
    gather_g[0].finish()
    gather_g[1].finish()
    for copy in started:
        copy.wait_send()


def collect(grad, factor, basis):
    slots = 2 * NZ
    chunk = pltpu.VMEM((CHUNKS, CROWS, 2048), BF16)
    dma = pltpu.SemaphoreType.DMA
    return pl.pallas_call(
        collect_kernel,
        out_shape=(
            jax.ShapeDtypeStruct((slots, ROWS, BLOCK), BF16),
            jax.ShapeDtypeStruct((slots, ROWS, WINDOW), F32),
            jax.ShapeDtypeStruct((slots, ROWS, BLOCK), BF16),
        ),
        in_specs=[pl.BlockSpec(memory_space=pltpu.HBM)] * 3,
        out_specs=(VMEM_SPEC,) * 3,
        scratch_shapes=[
            pltpu.VMEM(grad.shape, BF16),
            pltpu.VMEM(factor.shape, F32),
            pltpu.VMEM(basis.shape, F32),
        ]
        + [chunk] * 8
        + [
            pltpu.VMEM((NY, ROWS, HALF), BF16),
            pltpu.VMEM((NY - 1, ROWS, HALF), BF16),
            pltpu.VMEM((ROWS, HALF), BF16),
            dma((3,)),
        ]
        + [dma((CHUNKS, 2))] * 6
        + [dma((NY - 1, 2))] * 2
        + [dma((2,))] * 2
        + list(GATHER_SEMS) * 4,
        compiler_params=pltpu.CompilerParams(
            collective_id=0, has_side_effects=True, vmem_limit_bytes=VMEM_BYTES
        ),
        name="collect",
    )(*(pltpu.with_memory_space_constraint(a, pltpu.HBM) for a in (grad, factor, basis)))


def split(value):
    high = value.astype(BF16)
    return high, (value - high.astype(F32)).astype(BF16)


def dot3(left, right, numbers):
    dot = functools.partial(lax.dot_general, dimension_numbers=numbers, preferred_element_type=F32)
    return dot(left[0], right[0]) + (dot(left[0], right[1]) + dot(left[1], right[0]))


def factor_inverse(rows):
    count = len(rows)
    shape = rows[0].shape
    lane = lax.broadcasted_iota(jnp.int32, shape, 1)
    sub = lax.broadcasted_iota(jnp.int32, shape, 0)

    def along(value, column):
        return jnp.broadcast_to(value[:, column:column + 1], shape)

    def down(value, row):
        return jnp.broadcast_to(value[row:row + 1], shape)

    rows = list(rows)
    done = []
    columns = [along(rows[0], l) for l in range(8)]
    for group in range(count):
        base = 8 * group
        here = rows[group]
        more = group + 1 < count
        result = jnp.zeros(shape, F32)
        if more:
            below = rows[group + 1]
            below_columns = [along(below, base + l) for l in range(8)]
            next_columns = [along(below, base + 8 + l) for l in range(8)]
        for k in range(8):
            own = sub == k
            pivot = down(columns[k], k)
            inverse = 1.0 / pivot
            row = jnp.where(lane == base + k, 1.0, down(here, k))
            ahead = [down(columns[l], k) for l in range(k + 1, 8)]
            result = jnp.where(own, row * lax.rsqrt(pivot), result)
            scale = jnp.where(own, -inverse, columns[k] * inverse)
            here = jnp.where(own | (lane == base + k), 0.0, here) - scale * row
            for l in range(k + 1, 8):
                columns[l] = jnp.where(own, 0.0, columns[l]) - scale * ahead[l - k - 1]
            if more:
                scale = below_columns[k] * inverse
                below = jnp.where(lane == base + k, 0.0, below) - scale * row
                for l in range(k + 1, 8):
                    below_columns[l] = below_columns[l] - scale * ahead[l - k - 1]
                for l in range(8):
                    next_columns[l] = next_columns[l] - scale * down(below_columns[k], l)
        done.append(jnp.where(lane <= base + sub, result, 0.0))
        if more:
            rows[group + 1] = below
            columns = next_columns
        if group + 2 < count:
            spread = [down(here, l) for l in range(8)]
            inside = (lane >= base) & (lane < base + 8)
            near = min(group + 3, count)
            for n in range(group + 2, near):
                terms = [along(rows[n], base + l) * spread[l] for l in range(8)]
                while len(terms) > 1:
                    terms = [terms[i] + terms[i + 1] for i in range(0, len(terms), 2)]
                rows[n] = jnp.where(inside, 0.0, rows[n]) - terms[0]
            if near < count:
                far = jnp.concatenate(rows[near:], axis=0)
                lifted = [here if n == group else jnp.zeros(shape, F32) for n in range(count)]
                change = dot3(split(far), split(jnp.concatenate(lifted, axis=0)), NN)
                for n in range(near, count):
                    rows[n] = jnp.where(inside, 0.0, rows[n]) - change[8 * (n - near):8 * (n - near) + 8]
    return done


def refresh_kernel(
    grad, factor, basis, own_factor, first_old, second_old,
    new_factor, new_rows, new_first, new_second, direction,
    power, high, low, gram, upper, lower, basis_t, right_top, right_low, slab, left_rows,
    part, all_normal, weighted, weighted_in,
    send, recv, *gather_sems,
):
    x, y, z, core = place()
    me = z * 2 + core
    side = lax.rem(y, 2)
    tile = 256
    dp = x * NY + y
    partner = dp + 1 - 2 * side
    all_here = greet([
        (partner, me),
        (dp, lax.rem(z + 1, NZ) * 2 + core),
        (dp, lax.rem(z + NZ - 1, NZ) * 2 + core),
        (dp, z * 2 + 1 - core),
    ])

    def across(src, dst, i):
        return remote(src, dst, send.at[i], recv.at[i], partner, me)

    def dot(a, b, numbers):
        return lax.dot_general(a, b, numbers, preferred_element_type=F32)

    @pl.when(side == 0)
    def _():
        @pl.loop(0, BLOCK // tile)
        def _(i):
            rows = pl.ds(pl.multiple_of(i * tile, tile), tile)
            power[rows, :] = lax.dot_general(grad[rows, :], grad[...], NT, preferred_element_type=F32)

    @pl.when(side == 1)
    def _():
        @pl.loop(0, BLOCK // tile)
        def _(i):
            rows = pl.ds(pl.multiple_of(i * tile, tile), tile)
            power[rows, :] = lax.dot_general(grad[:, rows], grad[...], TN, preferred_element_type=F32)

    mine = pl.ds(pl.multiple_of(me * ROWS, ROWS), ROWS)
    new_factor[...] = 0.95 * own_factor[...] + 0.05 * power[mine, :]

    @pl.loop(0, NZ)
    def _(i):
        rows = pl.ds(pl.multiple_of(i * PANEL, PANEL), PANEL)
        for block in range(WINDOW // PANEL):
            columns = pl.ds(pl.multiple_of(lax.rem(i + block, NZ) * PANEL, PANEL), PANEL)
            now = 0.95 * factor[rows, block * PANEL:(block + 1) * PANEL] + 0.05 * power[rows, columns]
            high[rows, columns], low[rows, columns] = split(now)
            if 0 < block < NZ // 2:
                high[columns, rows], low[columns, rows] = split(now.T)

    @pl.loop(0, BLOCK // tile)
    def _(i):
        rows = pl.ds(pl.multiple_of(i * tile, tile), tile)
        now = basis[:, rows]
        power[rows, :] = lax.dot_general(
            now, high[...], TN, preferred_element_type=F32
        ) + lax.dot_general(now, low[...], TN, preferred_element_type=F32)

    def factored(dst, corner):
        rows = [gram[corner + 8 * i:corner + 8 * i + 8, corner:corner + PANEL] for i in range(PANEL // 8)]
        for i, value in enumerate(factor_inverse(rows)):
            dst[8 * i:8 * i + 8, :] = value
        return split(dst[...])

    top, bottom = slice(0, PANEL), slice(PANEL, 2 * PANEL)
    to_slab = across(basis_t.at[mine], slab, 4)
    to_rows = across(new_rows, left_rows, 5)

    def to_left(k):
        if k < 2:
            rows = pl.ds(k * tile, tile)
            return across(basis_t.at[rows], right_top.at[rows], k)
        rows, target = pl.ds(k * tile, tile), pl.ds((k - 2) * tile, tile)
        return across(basis_t.at[rows, 0:HALF], right_low.at[target], k)

    all_here()

    @pl.loop(0, BLOCK // tile)
    def _(k):
        rows = pl.ds(pl.multiple_of(k * tile, tile), tile)
        panel = split(power[rows, :])
        gram[...] = dot3(panel, panel, NT)
        first = factored(upper, 0)
        below = split(dot3(split(gram[bottom, top]), first, NT))
        gram[bottom, bottom] = gram[bottom, bottom] - dot3(below, below, NT)
        cross = split(dot3(below, first, NN))
        second = factored(lower, PANEL)
        gram[top, top] = upper[...]
        gram[top, bottom] = jnp.zeros((PANEL, PANEL), F32)
        gram[bottom, top] = -dot3(second, cross, NN)
        gram[bottom, bottom] = lower[...]
        fresh = dot3(split(gram[...]), panel, NN)
        basis_t[rows, :] = fresh.astype(BF16)
        for panel_index in range(BLOCK // tile):
            @pl.when((side == 1) & (k == panel_index))
            def _():
                to_left(panel_index).start()

        @pl.when((side == 0) & (k == me // 4))
        def _():
            to_slab.start()

        fresh = split(fresh)

        @pl.loop(k + 1, BLOCK // tile)
        def _(j):
            later = pl.ds(pl.multiple_of(j * tile, tile), tile)
            old = power[later, :]
            overlap = dot3(split(old), fresh, NT)
            power[later, :] = old - dot3(split(overlap), fresh, NN)

    pick = lax.broadcasted_iota(jnp.int32, (ROWS, BLOCK), 1) == me * ROWS + lax.broadcasted_iota(
        jnp.int32, (ROWS, BLOCK), 0
    )
    new_rows[...] = lax.dot_general(
        pick.astype(BF16), basis_t[...], NT, preferred_element_type=F32
    ).astype(BF16)


    count = ROWS // 2
    halves = [pl.ds(h * count, count) for h in range(2)]
    to_weighted = [across(weighted.at[r], weighted_in.at[r], 6 + h) for h, r in enumerate(halves)]
    gathers = [
        Gather(None, all_normal, *gather_sems[4 * h:4 * h + 4], h * count, count) for h in range(2)
    ]

    @pl.when(side == 0)
    def _():
        to_rows.start()
        slab[...] = basis_t[mine, :]
        left_rows[...] = new_rows[...]
        mixed = dot(slab[...], grad[...], NN).astype(BF16)
        to_left(0).wait_recv()
        to_left(1).wait_recv()
        part[...] = dot(mixed, right_top[...], NT)

    @pl.when(side == 1)
    def _():
        to_slab.wait_recv()
        mixed = dot(slab[...], grad[...], NN).astype(BF16)
        part[...] = dot(mixed, basis_t[HALF:BLOCK, :], NT)

    for h, rows in enumerate(halves):
        rotated = part[rows, :]
        first_now = 0.95 * first_old[rows, :] + 0.05 * rotated
        second_now = 0.95 * second_old[rows, :] + 0.05 * rotated * rotated
        all_normal[me, rows] = (first_now / (jnp.sqrt(second_now) + 1e-08)).astype(BF16)
        gathers[h].begin()
        new_first[rows, :] = first_now
        new_second[rows, :] = second_now

    for step in range(1, NZ // 2 + 1):
        for gather in gathers:
            gather.advance(step)
    for gather in gathers:
        gather.finish()

    @pl.when(side == 1)
    def _():
        to_rows.wait_recv()

    weighted[...] = dot(left_rows[...], all_normal[...].reshape(BLOCK, HALF), NN).astype(BF16)
    for copy in to_weighted:
        copy.start()

    @pl.when(side == 0)
    def _():
        to_left(2).wait_recv()
        to_left(3).wait_recv()
        own = dot(weighted[...], right_top[:, 0:HALF], NN)
        for copy in to_weighted:
            copy.wait_recv()
        direction[...] = (own + dot(weighted_in[...], right_low[...], NN)).astype(BF16)
        to_slab.wait_send()
        to_rows.wait_send()

    @pl.when(side == 1)
    def _():
        own = dot(weighted[...], basis_t[HALF:BLOCK, HALF:BLOCK], NN)
        for copy in to_weighted:
            copy.wait_recv()
        direction[...] = (own + dot(weighted_in[...], basis_t[0:HALF, HALF:BLOCK], NN)).astype(BF16)
        for k in range(4):
            to_left(k).wait_send()

    for copy in to_weighted:
        copy.wait_send()


def refresh(grad, factor, basis, own_factor, first, second):
    dma = pltpu.SemaphoreType.DMA
    return pl.pallas_call(
        refresh_kernel,
        out_shape=(
            jax.ShapeDtypeStruct((ROWS, BLOCK), F32),
            jax.ShapeDtypeStruct((ROWS, BLOCK), BF16),
            jax.ShapeDtypeStruct((ROWS, HALF), F32),
            jax.ShapeDtypeStruct((ROWS, HALF), F32),
            jax.ShapeDtypeStruct((ROWS, HALF), BF16),
        ),
        in_specs=[VMEM_SPEC] * 6,
        out_specs=(VMEM_SPEC,) * 5,
        scratch_shapes=[
            pltpu.VMEM((BLOCK, BLOCK), F32),
            pltpu.VMEM((BLOCK, BLOCK), BF16),
            pltpu.VMEM((BLOCK, BLOCK), BF16),
            pltpu.VMEM((2 * PANEL, 2 * PANEL), F32),
            pltpu.VMEM((PANEL, PANEL), F32),
            pltpu.VMEM((PANEL, PANEL), F32),
            pltpu.VMEM((BLOCK, BLOCK), BF16),
            pltpu.VMEM((HALF, BLOCK), BF16),
            pltpu.VMEM((HALF, HALF), BF16),
            pltpu.VMEM((ROWS, BLOCK), BF16),
            pltpu.VMEM((ROWS, BLOCK), BF16),
            pltpu.VMEM((ROWS, HALF), F32),
            pltpu.VMEM((2 * NZ, ROWS, HALF), BF16),
            pltpu.VMEM((ROWS, HALF), BF16),
            pltpu.VMEM((ROWS, HALF), BF16),
            dma((8,)),
            dma((8,)),
            *GATHER_SEMS,
            *GATHER_SEMS,
        ],
        compiler_params=pltpu.CompilerParams(
            collective_id=1, has_side_effects=True, vmem_limit_bytes=VMEM_BYTES
        ),
        name="refresh",
    )(grad, factor, basis, own_factor, first, second)


def finish_kernel(*refs):
    count = len(refs) // 2
    for source, target in zip(refs[:count], refs[count:]):
        target[...] = source[...]


def finish(*arrays):
    return pl.pallas_call(
        finish_kernel,
        out_shape=tuple(jax.ShapeDtypeStruct(a.shape, a.dtype) for a in arrays),
        in_specs=[VMEM_SPEC] * len(arrays),
        out_specs=(VMEM_SPEC,) * len(arrays),
        compiler_params=pltpu.CompilerParams(vmem_limit_bytes=8 << 20),
        name="finish",
    )(*arrays)


def body(grad_partial, factors, bases, first_moment, second_moment):
    all_grad, all_factor, all_basis = collect(grad_partial[0], factors[0], bases[0])
    whole = (BLOCK, BLOCK)
    all_grad = all_grad.reshape(whole)
    new_factor, new_rows, first_new, second_new, direction = finish(
        *refresh(
            all_grad, all_factor.reshape(BLOCK, WINDOW), all_basis.reshape(whole),
            factors[0], first_moment[0], second_moment[0],
        )
    )
    return (new_factor[None], new_rows[None], first_new[None], second_new[None], direction[None])


def solution(mesh):
    spec = P("dp", "fsdp", None)
    return jax.shard_map(
        body,
        mesh=mesh,
        in_specs=(P("dp", None, "fsdp", None), spec, spec, spec, spec),
        out_specs=(spec,) * 5,
        check_vma=False,
    )
```

```python
import functools

import jax
import jax.numpy as jnp
from jax import lax
from jax.experimental import pallas as pl
from jax.experimental.pallas import tpu as pltpu
from jax.sharding import PartitionSpec as P

F32 = jnp.float32
BF16 = jnp.bfloat16
NN = (((1,), (0,)), ((), ()))
NT = (((1,), (1,)), ((), ()))
TN = (((0,), (0,)), ((), ()))
NX, NY, NZ = 4, 8, 8
ROWS = 64
BLOCK = 1024
HALF = 512
CHUNKS = 4
CROWS = ROWS // CHUNKS
PARTS = ((0, 3 * CROWS), (3 * CROWS, CROWS))
PANEL = 128
WINDOW = 5 * PANEL
VMEM_SPEC = pl.BlockSpec(memory_space=pltpu.VMEM)
VMEM_BYTES = 40 << 20


def place():
    dp = lax.axis_index("dp")
    fsdp = lax.axis_index("fsdp")
    return dp // NY, lax.rem(dp, NY), fsdp // 2, lax.rem(fsdp, 2)


def remote(src, dst, send, recv, dp, fsdp):
    return pltpu.make_async_remote_copy(
        src_ref=src,
        dst_ref=dst,
        send_sem=send,
        recv_sem=recv,
        device_id={"dp": dp, "fsdp": fsdp},
        device_id_type=pl.DeviceIdType.MESH,
    )


def greet(peers):
    barrier = pltpu.get_barrier_semaphore()
    for dp, fsdp in peers:
        pl.semaphore_signal(
            barrier,
            inc=1,
            device_id={"dp": dp, "fsdp": fsdp},
            device_id_type=pl.DeviceIdType.MESH,
        )
    return lambda: pl.semaphore_wait(barrier, len(peers))


def meet(peers):
    greet(peers)()


class Gather:
    def __init__(self, own, held, send, recv, hand_send, hand_recv, start=0, count=ROWS):
        self.own, self.held = own, held
        self.start, self.count = start, count
        self.send, self.recv = send, recv
        self.hand_send, self.hand_recv = hand_send, hand_recv
        self.x, self.y, self.z, self.core = place()
        self.dp = self.x * NY + self.y
        self.started = []

    def ways(self, step):
        return (0, 1) if step < NZ // 2 or self.count % (2 * CROWS) == 0 else (0,)

    def slot(self, z, core):
        return lax.rem(z + NZ, NZ) * 2 + core

    def part(self, z, core, step, way):
        start, count = self.start, self.count
        if len(self.ways(step)) == 2 and step == NZ // 2:
            count = count // 2
            start = start + way * count
        return self.held.at[self.slot(z, core), pl.ds(start, count)]

    def hop(self, step, way):
        sign = 1 - 2 * way
        origin = self.z - sign * (step - 1)
        target = self.slot(self.z + sign, self.core)
        dst = self.part(origin, self.core, step, way)
        src = self.own if step == 1 and self.own is not None else dst
        return remote(
            src, dst, self.send.at[step - 1, way], self.recv.at[step - 1, way], self.dp, target
        )

    def hand(self, item, view, core):
        src = view if item or self.own is None else self.own
        return remote(
            src if core is None else view,
            view,
            self.hand_send.at[item],
            self.hand_recv.at[item],
            self.dp,
            self.slot(self.z, 1 - self.core),
        )

    def begin(self):
        for way in range(2):
            copy = self.hop(1, way)
            copy.start()
            self.started.append(copy)
        copy = self.hand(0, self.part(self.z, self.core, 1, 0), None)
        copy.start()
        self.started.append(copy)

    def advance(self, step):
        for way in self.ways(step):
            sign = 1 - 2 * way
            view = self.part(self.z - sign * step, self.core, step, way)
            remote(
                view,
                view,
                self.send.at[step - 1, way],
                self.recv.at[step - 1, way],
                self.dp,
                self.slot(self.z + sign, self.core),
            ).wait_recv()
            if step < NZ // 2 and way in self.ways(step + 1):
                copy = self.hop(step + 1, way)
                copy.start()
                self.started.append(copy)
            copy = self.hand(1 + 2 * (step - 1) + way, view, None)
            copy.start()
            self.started.append(copy)

    def finish(self):
        other = 1 - self.core
        self.hand(0, self.part(self.z, other, 1, 0), other).wait_recv()
        for step in range(1, NZ // 2 + 1):
            for way in self.ways(step):
                sign = 1 - 2 * way
                view = self.part(self.z - sign * step, other, step, way)
                self.hand(1 + 2 * (step - 1) + way, view, other).wait_recv()
        for copy in self.started:
            copy.wait_send()


GATHER_SEMS = (
    pltpu.SemaphoreType.DMA((NZ // 2, 2)),
    pltpu.SemaphoreType.DMA((NZ // 2, 2)),
    pltpu.SemaphoreType.DMA((NZ + 1,)),
    pltpu.SemaphoreType.DMA((NZ + 1,)),
)


def collect_kernel(
    grad_hbm, factor_hbm, basis_hbm, all_grad, all_factor, all_basis,
    grad, factor, basis, first_right, first_left, sum_right, sum_left,
    right_a, right_b, left_a, left_b, lane_sum, lane_in, half_out,
    own_sem,
    s1, r1, s2, r2, s3, r3, ys, yr, ex_send, ex_recv,
    *gather_sems,
):
    x, y, z, core = place()
    me = z * 2 + core
    side = lax.rem(y, 2)
    dp = x * NY + y
    right = lax.rem(x + 1, NX) * NY + y
    left = lax.rem(x + NX - 1, NX) * NY + y
    partner = x * NY + y + 1 - 2 * side
    peers = [(right, me), (left, me)]
    peers += [(x * NY + lax.rem(y + d, NY), me) for d in range(1, NY)]
    peers += [
        (dp, lax.rem(z + 1, NZ) * 2 + core),
        (dp, lax.rem(z + NZ - 1, NZ) * 2 + core),
        (dp, z * 2 + 1 - core),
    ]
    staged = [
        pltpu.make_async_copy(src, dst, own_sem.at[i])
        for i, (src, dst) in enumerate(((grad_hbm, grad), (basis_hbm, basis), (factor_hbm, factor)))
    ]
    for copy in staged:
        copy.start()
    meet(peers)
    staged[0].wait()

    def region(owner, part, chunk):
        owner = lax.rem(owner + NX, NX)
        start = pl.multiple_of(lax.rem(owner, 2) * 4096 + part * 2048, 2048)
        return owner // 2, pl.ds(chunk * CROWS, CROWS), pl.ds(start, 2048)

    started = []

    def begin(copy):
        copy.start()
        started.append(copy)
        return copy

    for r in range(CHUNKS):
        begin(remote(grad.at[region(x + 2, 0, r)], first_right.at[r], s1.at[r, 0], r1.at[r, 0], right, me))
        begin(remote(grad.at[region(x - 2, 1, r)], first_left.at[r], s1.at[r, 1], r1.at[r, 1], left, me))
    gather_b = Gather(None, all_basis, *gather_sems[0:4])
    gather_f = Gather(None, all_factor, *gather_sems[4:8])
    gather_g = [
        Gather(None, all_grad, *gather_sems[8 + 4 * h:12 + 4 * h], *PARTS[h]) for h in range(2)
    ]
    staged[1].wait()
    all_basis[me] = basis[...].astype(BF16)
    gather_b.begin()
    staged[2].wait()
    for block in range(WINDOW // PANEL):
        start = pl.multiple_of(lax.rem(z + block, NZ) * PANEL, PANEL)
        all_factor[me, :, block * PANEL:(block + 1) * PANEL] = factor[:, pl.ds(start, PANEL)]
    gather_f.begin()

    def forward(r):
        remote(first_right.at[r], first_right.at[r], s1.at[r, 0], r1.at[r, 0], right, me).wait_recv()
        own = grad[region(x + 1, 0, r)].astype(F32)
        sum_right[r] = (own + first_right[r].astype(F32)).astype(BF16)
        begin(remote(sum_right.at[r], right_a.at[r], s2.at[r, 0], r2.at[r, 0], right, me))
        begin(remote(grad.at[region(x + 1, 1, r)], right_b.at[r], s3.at[r, 0], r3.at[r, 0], right, me))
        remote(first_left.at[r], first_left.at[r], s1.at[r, 1], r1.at[r, 1], left, me).wait_recv()
        own = grad[region(x - 1, 1, r)].astype(F32)
        sum_left[r] = (own + first_left[r].astype(F32)).astype(BF16)
        begin(remote(sum_left.at[r], left_b.at[r], s2.at[r, 1], r2.at[r, 1], left, me))
        begin(remote(grad.at[region(x - 1, 0, r)], left_a.at[r], s3.at[r, 1], r3.at[r, 1], left, me))

    def turn(r):
        remote(right_a.at[r], right_a.at[r], s2.at[r, 0], r2.at[r, 0], right, me).wait_recv()
        remote(right_b.at[r], right_b.at[r], s3.at[r, 0], r3.at[r, 0], right, me).wait_recv()
        remote(left_b.at[r], left_b.at[r], s2.at[r, 1], r2.at[r, 1], left, me).wait_recv()
        remote(left_a.at[r], left_a.at[r], s3.at[r, 1], r3.at[r, 1], left, me).wait_recv()
        rows = pl.ds(r * CROWS, CROWS)
        for part, (from_left, from_right) in enumerate(((right_a, left_a), (right_b, left_b))):
            total = grad[region(x, part, r)].astype(F32)
            total = total + from_left[r].astype(F32) + from_right[r].astype(F32)
            total = total.astype(BF16)
            for piece in range(4):
                lane_sum[part * 4 + piece, rows] = total[:, piece * HALF:(piece + 1) * HALF]
        for d in range(1, NY):
            target = lax.rem(y + d, NY)
            begin(remote(
                lane_sum.at[target, rows], lane_in.at[d - 1, rows],
                ys.at[d - 1, r], yr.at[d - 1, r], x * NY + target, me,
            ))

    mine = pl.ds(pl.multiple_of(side * HALF, HALF), HALF)
    theirs = pl.ds(pl.multiple_of((1 - side) * HALF, HALF), HALF)

    def land(h):
        rows = pl.ds(*PARTS[h])
        total = lane_sum[y, rows].astype(F32)
        for r in range(PARTS[h][0] // CROWS, sum(PARTS[h]) // CROWS):
            for d in range(1, NY):
                view = lane_in.at[d - 1, pl.ds(r * CROWS, CROWS)]
                remote(view, view, ys.at[d - 1, r], yr.at[d - 1, r], x * NY + lax.rem(y + d, NY), me).wait_recv()
        for d in range(1, NY):
            total = total + lane_in[d - 1, rows].astype(F32)
        total = total.astype(BF16)
        half_out[rows] = total
        all_grad[me, rows, mine] = total
        begin(remote(half_out.at[rows], all_grad.at[me, rows, mine], ex_send.at[h], ex_recv.at[h], partner, me))

    def paired(h):
        view = all_grad.at[me, pl.ds(*PARTS[h]), theirs]
        remote(view, view, ex_send.at[h], ex_recv.at[h], partner, me).wait_recv()
        gather_g[h].begin()

    forward(0)
    forward(1)
    gather_b.advance(1)
    forward(2)
    forward(3)
    gather_f.advance(1)
    turn(0)
    gather_b.advance(2)
    turn(1)
    gather_f.advance(2)
    turn(2)
    gather_b.advance(3)
    turn(3)
    gather_f.advance(3)
    land(0)
    gather_b.advance(4)
    paired(0)
    land(1)
    gather_f.advance(4)
    paired(1)
    for step in range(1, NZ // 2 + 1):
        gather_g[0].advance(step)
        gather_g[1].advance(step)
    gather_b.finish()
    gather_f.finish()
    gather_g[0].finish()
    gather_g[1].finish()
    for copy in started:
        copy.wait_send()


def collect(grad, factor, basis):
    slots = 2 * NZ
    chunk = pltpu.VMEM((CHUNKS, CROWS, 2048), BF16)
    dma = pltpu.SemaphoreType.DMA
    return pl.pallas_call(
        collect_kernel,
        out_shape=(
            jax.ShapeDtypeStruct((slots, ROWS, BLOCK), BF16),
            jax.ShapeDtypeStruct((slots, ROWS, WINDOW), F32),
            jax.ShapeDtypeStruct((slots, ROWS, BLOCK), BF16),
        ),
        in_specs=[pl.BlockSpec(memory_space=pltpu.HBM)] * 3,
        out_specs=(VMEM_SPEC,) * 3,
        scratch_shapes=[
            pltpu.VMEM(grad.shape, BF16),
            pltpu.VMEM(factor.shape, F32),
            pltpu.VMEM(basis.shape, F32),
        ]
        + [chunk] * 8
        + [
            pltpu.VMEM((NY, ROWS, HALF), BF16),
            pltpu.VMEM((NY - 1, ROWS, HALF), BF16),
            pltpu.VMEM((ROWS, HALF), BF16),
            dma((3,)),
        ]
        + [dma((CHUNKS, 2))] * 6
        + [dma((NY - 1, CHUNKS))] * 2
        + [dma((2,))] * 2
        + list(GATHER_SEMS) * 4,
        compiler_params=pltpu.CompilerParams(
            collective_id=0, has_side_effects=True, vmem_limit_bytes=VMEM_BYTES
        ),
        name="collect",
    )(*(pltpu.with_memory_space_constraint(a, pltpu.HBM) for a in (grad, factor, basis)))


def split(value):
    high = value.astype(BF16)
    return high, (value - high.astype(F32)).astype(BF16)


def dot3(left, right, numbers):
    dot = functools.partial(lax.dot_general, dimension_numbers=numbers, preferred_element_type=F32)
    return dot(left[0], right[0]) + (dot(left[0], right[1]) + dot(left[1], right[0]))


def factor_inverse(rows):
    count = len(rows)
    shape = rows[0].shape
    lane = lax.broadcasted_iota(jnp.int32, shape, 1)
    sub = lax.broadcasted_iota(jnp.int32, shape, 0)

    def along(value, column):
        return jnp.broadcast_to(value[:, column:column + 1], shape)

    def down(value, row):
        return jnp.broadcast_to(value[row:row + 1], shape)

    rows = list(rows)
    done = []
    columns = [along(rows[0], l) for l in range(8)]
    for group in range(count):
        base = 8 * group
        here = rows[group]
        more = group + 1 < count
        result = jnp.zeros(shape, F32)
        if more:
            below = rows[group + 1]
            below_columns = [along(below, base + l) for l in range(8)]
            next_columns = [along(below, base + 8 + l) for l in range(8)]
        for k in range(8):
            own = sub == k
            pivot = down(columns[k], k)
            inverse = 1.0 / pivot
            row = jnp.where(lane == base + k, 1.0, down(here, k))
            ahead = [down(columns[l], k) for l in range(k + 1, 8)]
            result = jnp.where(own, row * lax.rsqrt(pivot), result)
            scale = jnp.where(own, -inverse, columns[k] * inverse)
            here = jnp.where(own | (lane == base + k), 0.0, here) - scale * row
            for l in range(k + 1, 8):
                columns[l] = jnp.where(own, 0.0, columns[l]) - scale * ahead[l - k - 1]
            if more:
                scale = below_columns[k] * inverse
                below = jnp.where(lane == base + k, 0.0, below) - scale * row
                for l in range(k + 1, 8):
                    below_columns[l] = below_columns[l] - scale * ahead[l - k - 1]
                for l in range(8):
                    next_columns[l] = next_columns[l] - scale * down(below_columns[k], l)
        done.append(jnp.where(lane <= base + sub, result, 0.0))
        if more:
            rows[group + 1] = below
            columns = next_columns
        if group + 2 < count:
            spread = [down(here, l) for l in range(8)]
            inside = (lane >= base) & (lane < base + 8)
            near = min(group + 3, count)
            for n in range(group + 2, near):
                terms = [along(rows[n], base + l) * spread[l] for l in range(8)]
                while len(terms) > 1:
                    terms = [terms[i] + terms[i + 1] for i in range(0, len(terms), 2)]
                rows[n] = jnp.where(inside, 0.0, rows[n]) - terms[0]
            if near < count:
                far = jnp.concatenate(rows[near:], axis=0)
                lifted = [here if n == group else jnp.zeros(shape, F32) for n in range(count)]
                change = dot3(split(far), split(jnp.concatenate(lifted, axis=0)), NN)
                for n in range(near, count):
                    rows[n] = jnp.where(inside, 0.0, rows[n]) - change[8 * (n - near):8 * (n - near) + 8]
    return done


def refresh_kernel(
    grad, factor, basis, own_factor, first_old, second_old,
    new_factor, new_rows, new_first, new_second, direction,
    power, high, low, gram, upper, lower, basis_t, right_top, right_low, slab, left_rows,
    part, all_normal, weighted, weighted_in,
    send, recv, *gather_sems,
):
    x, y, z, core = place()
    me = z * 2 + core
    side = lax.rem(y, 2)
    tile = 256
    dp = x * NY + y
    partner = dp + 1 - 2 * side
    all_here = greet([
        (partner, me),
        (dp, lax.rem(z + 1, NZ) * 2 + core),
        (dp, lax.rem(z + NZ - 1, NZ) * 2 + core),
        (dp, z * 2 + 1 - core),
    ])

    def across(src, dst, i):
        return remote(src, dst, send.at[i], recv.at[i], partner, me)

    def dot(a, b, numbers):
        return lax.dot_general(a, b, numbers, preferred_element_type=F32)

    @pl.when(side == 0)
    def _():
        @pl.loop(0, BLOCK // tile)
        def _(i):
            rows = pl.ds(pl.multiple_of(i * tile, tile), tile)
            power[rows, :] = lax.dot_general(grad[rows, :], grad[...], NT, preferred_element_type=F32)

    @pl.when(side == 1)
    def _():
        @pl.loop(0, BLOCK // tile)
        def _(i):
            rows = pl.ds(pl.multiple_of(i * tile, tile), tile)
            power[rows, :] = lax.dot_general(grad[:, rows], grad[...], TN, preferred_element_type=F32)

    mine = pl.ds(pl.multiple_of(me * ROWS, ROWS), ROWS)
    new_factor[...] = 0.95 * own_factor[...] + 0.05 * power[mine, :]

    @pl.loop(0, NZ)
    def _(i):
        rows = pl.ds(pl.multiple_of(i * PANEL, PANEL), PANEL)
        for block in range(WINDOW // PANEL):
            columns = pl.ds(pl.multiple_of(lax.rem(i + block, NZ) * PANEL, PANEL), PANEL)
            now = 0.95 * factor[rows, block * PANEL:(block + 1) * PANEL] + 0.05 * power[rows, columns]
            high[rows, columns], low[rows, columns] = split(now)
            if 0 < block < NZ // 2:
                high[columns, rows], low[columns, rows] = split(now.T)

    @pl.loop(0, BLOCK // tile)
    def _(i):
        rows = pl.ds(pl.multiple_of(i * tile, tile), tile)
        now = basis[:, rows]
        power[rows, :] = lax.dot_general(
            now, high[...], TN, preferred_element_type=F32
        ) + lax.dot_general(now, low[...], TN, preferred_element_type=F32)

    def factored(dst, corner):
        rows = [gram[corner + 8 * i:corner + 8 * i + 8, corner:corner + PANEL] for i in range(PANEL // 8)]
        for i, value in enumerate(factor_inverse(rows)):
            dst[8 * i:8 * i + 8, :] = value
        return split(dst[...])

    top, bottom = slice(0, PANEL), slice(PANEL, 2 * PANEL)
    to_slab = across(basis_t.at[mine], slab, 4)
    to_rows = across(new_rows, left_rows, 5)

    def to_left(k):
        if k < 2:
            rows = pl.ds(k * tile, tile)
            return across(basis_t.at[rows], right_top.at[rows], k)
        rows, target = pl.ds(k * tile, tile), pl.ds((k - 2) * tile, tile)
        return across(basis_t.at[rows, 0:HALF], right_low.at[target], k)

    all_here()

    @pl.loop(0, BLOCK // tile)
    def _(k):
        rows = pl.ds(pl.multiple_of(k * tile, tile), tile)
        panel = split(power[rows, :])
        gram[...] = dot3(panel, panel, NT)
        first = factored(upper, 0)
        below = split(dot3(split(gram[bottom, top]), first, NT))
        gram[bottom, bottom] = gram[bottom, bottom] - dot3(below, below, NT)
        cross = split(dot3(below, first, NN))
        second = factored(lower, PANEL)
        gram[top, top] = upper[...]
        gram[top, bottom] = jnp.zeros((PANEL, PANEL), F32)
        gram[bottom, top] = -dot3(second, cross, NN)
        gram[bottom, bottom] = lower[...]
        fresh = dot3(split(gram[...]), panel, NN)
        basis_t[rows, :] = fresh.astype(BF16)
        for panel_index in range(BLOCK // tile):
            @pl.when((side == 1) & (k == panel_index))
            def _():
                to_left(panel_index).start()

        @pl.when((side == 0) & (k == me // 4))
        def _():
            to_slab.start()

        fresh = split(fresh)

        @pl.loop(k + 1, BLOCK // tile)
        def _(j):
            later = pl.ds(pl.multiple_of(j * tile, tile), tile)
            old = power[later, :]
            overlap = dot3(split(old), fresh, NT)
            power[later, :] = old - dot3(split(overlap), fresh, NN)

    pick = lax.broadcasted_iota(jnp.int32, (ROWS, BLOCK), 1) == me * ROWS + lax.broadcasted_iota(
        jnp.int32, (ROWS, BLOCK), 0
    )
    new_rows[...] = lax.dot_general(
        pick.astype(BF16), basis_t[...], NT, preferred_element_type=F32
    ).astype(BF16)


    count = ROWS // 2
    halves = [pl.ds(h * count, count) for h in range(2)]
    to_weighted = [across(weighted.at[r], weighted_in.at[r], 6 + h) for h, r in enumerate(halves)]
    gathers = [
        Gather(None, all_normal, *gather_sems[4 * h:4 * h + 4], h * count, count) for h in range(2)
    ]

    @pl.when(side == 0)
    def _():
        to_rows.start()
        slab[...] = basis_t[mine, :]
        left_rows[...] = new_rows[...]
        mixed = dot(slab[...], grad[...], NN).astype(BF16)
        to_left(0).wait_recv()
        to_left(1).wait_recv()
        part[...] = dot(mixed, right_top[...], NT)

    @pl.when(side == 1)
    def _():
        to_slab.wait_recv()
        mixed = dot(slab[...], grad[...], NN).astype(BF16)
        part[...] = dot(mixed, basis_t[HALF:BLOCK, :], NT)

    for h, rows in enumerate(halves):
        rotated = part[rows, :]
        first_now = 0.95 * first_old[rows, :] + 0.05 * rotated
        second_now = 0.95 * second_old[rows, :] + 0.05 * rotated * rotated
        all_normal[me, rows] = (first_now / (jnp.sqrt(second_now) + 1e-08)).astype(BF16)
        gathers[h].begin()
        new_first[rows, :] = first_now
        new_second[rows, :] = second_now

    for step in range(1, NZ // 2 + 1):
        for gather in gathers:
            gather.advance(step)
    for gather in gathers:
        gather.finish()

    @pl.when(side == 1)
    def _():
        to_rows.wait_recv()

    weighted[...] = dot(left_rows[...], all_normal[...].reshape(BLOCK, HALF), NN).astype(BF16)
    for copy in to_weighted:
        copy.start()

    @pl.when(side == 0)
    def _():
        to_left(2).wait_recv()
        to_left(3).wait_recv()
        own = dot(weighted[...], right_top[:, 0:HALF], NN)
        for copy in to_weighted:
            copy.wait_recv()
        direction[...] = (own + dot(weighted_in[...], right_low[...], NN)).astype(BF16)
        to_slab.wait_send()
        to_rows.wait_send()

    @pl.when(side == 1)
    def _():
        own = dot(weighted[...], basis_t[HALF:BLOCK, HALF:BLOCK], NN)
        for copy in to_weighted:
            copy.wait_recv()
        direction[...] = (own + dot(weighted_in[...], basis_t[0:HALF, HALF:BLOCK], NN)).astype(BF16)
        for k in range(4):
            to_left(k).wait_send()

    for copy in to_weighted:
        copy.wait_send()


def refresh(grad, factor, basis, own_factor, first, second):
    dma = pltpu.SemaphoreType.DMA
    return pl.pallas_call(
        refresh_kernel,
        out_shape=(
            jax.ShapeDtypeStruct((ROWS, BLOCK), F32),
            jax.ShapeDtypeStruct((ROWS, BLOCK), BF16),
            jax.ShapeDtypeStruct((ROWS, HALF), F32),
            jax.ShapeDtypeStruct((ROWS, HALF), F32),
            jax.ShapeDtypeStruct((ROWS, HALF), BF16),
        ),
        in_specs=[VMEM_SPEC] * 6,
        out_specs=(VMEM_SPEC,) * 5,
        scratch_shapes=[
            pltpu.VMEM((BLOCK, BLOCK), F32),
            pltpu.VMEM((BLOCK, BLOCK), BF16),
            pltpu.VMEM((BLOCK, BLOCK), BF16),
            pltpu.VMEM((2 * PANEL, 2 * PANEL), F32),
            pltpu.VMEM((PANEL, PANEL), F32),
            pltpu.VMEM((PANEL, PANEL), F32),
            pltpu.VMEM((BLOCK, BLOCK), BF16),
            pltpu.VMEM((HALF, BLOCK), BF16),
            pltpu.VMEM((HALF, HALF), BF16),
            pltpu.VMEM((ROWS, BLOCK), BF16),
            pltpu.VMEM((ROWS, BLOCK), BF16),
            pltpu.VMEM((ROWS, HALF), F32),
            pltpu.VMEM((2 * NZ, ROWS, HALF), BF16),
            pltpu.VMEM((ROWS, HALF), BF16),
            pltpu.VMEM((ROWS, HALF), BF16),
            dma((8,)),
            dma((8,)),
            *GATHER_SEMS,
            *GATHER_SEMS,
        ],
        compiler_params=pltpu.CompilerParams(
            collective_id=1, has_side_effects=True, vmem_limit_bytes=VMEM_BYTES
        ),
        name="refresh",
    )(grad, factor, basis, own_factor, first, second)


def finish_kernel(*refs):
    count = len(refs) // 2
    for source, target in zip(refs[:count], refs[count:]):
        target[...] = source[...]


def finish(*arrays):
    return pl.pallas_call(
        finish_kernel,
        out_shape=tuple(jax.ShapeDtypeStruct(a.shape, a.dtype) for a in arrays),
        in_specs=[VMEM_SPEC] * len(arrays),
        out_specs=(VMEM_SPEC,) * len(arrays),
        compiler_params=pltpu.CompilerParams(vmem_limit_bytes=8 << 20),
        name="finish",
    )(*arrays)


def body(grad_partial, factors, bases, first_moment, second_moment):
    all_grad, all_factor, all_basis = collect(grad_partial[0], factors[0], bases[0])
    whole = (BLOCK, BLOCK)
    all_grad = all_grad.reshape(whole)
    new_factor, new_rows, first_new, second_new, direction = finish(
        *refresh(
            all_grad, all_factor.reshape(BLOCK, WINDOW), all_basis.reshape(whole),
            factors[0], first_moment[0], second_moment[0],
        )
    )
    return (new_factor[None], new_rows[None], first_new[None], second_new[None], direction[None])


def solution(mesh):
    spec = P("dp", "fsdp", None)
    return jax.shard_map(
        body,
        mesh=mesh,
        in_specs=(P("dp", None, "fsdp", None), spec, spec, spec, spec),
        out_specs=(spec,) * 5,
        check_vma=False,
    )
```
